32 devices in a mesh: view: 8 (over z, core), span: 4 (over y, x).
Axes of the slice: x: 2, y: 2, z: 4, core: 2. Of those that a mesh axis runs over, the one named last changes fastest.
Arguments:
- tokens: bfloat16 [8, 1024, 1024], P('view', 'span'), may hold values from -6 to 6
- scan_order: int32 [8, 1024], P('view'), may hold values from 0 to 1023, as said below
- w_merge: bfloat16 [4096, 1024], replicated, may hold values from -0.09375 to 0.09375
- bias: bfloat16 [1024], replicated, may hold values from -4 to 4
- cotangent: bfloat16 [8, 256, 1024], P('view', 'span'), may hold values from -6 to 6
Outputs:
- merged_out: bfloat16 [8, 256, 1024], P('view', 'span')
- token_grad: bfloat16 [8, 1024, 1024], P('view', 'span')
- weight_grad: float32 [4096, 1024], P(('view', 'span'))
- bias_grad: float32 [1024], replicated
The draws below stay inside these ranges and needn't reach their ends.
Inputs may be any that keep to these rules, and one draw needn't show every extreme that they name: `scan_order`: each row is a permutation of the raster indices of one view. Call tokens 256 * b to 256 * (b + 1) - 1 band b, and scan positions 256 * c to 256 * (c + 1) - 1 block c: every block holds at most 96 tokens of any band, and in every row each block holds exactly 96 tokens of some band.
All inputs are finite; a program needn't handle non-finite values.
Results may differ from the reference program's by a relative error of at most 0.001.
Values may be sent and summed in bfloat16 or wider, within the bound.
No kernel may reach another device: no remote copies, remote signals or barrier semaphores. Data moves between devices by JAX's collectives and lax.ppermute only.
A program may use at most 128 MiB of HBM per device.

```python
import math
import jax
import jax.numpy as jnp
from jax import lax

DM = 1024
DO = 1024
MERGE_IN = 4096
COLS = 128
VIEWS = 8
ROWS = 8
TOK_DEV = 256
TOK_VIEW = 1024
MTOK_VIEW = 256
N_SPAN = 4


def scan_one_view(key):
    spans = N_SPAN
    base = TOK_DEV // spans
    half = base // 2
    key_a, key_b, key_c, key_d = jax.random.split(key, 4)
    first = jax.random.permutation(key_a, spans)
    offset = jax.random.randint(key_b, (), 1, spans)
    second = (first + offset) % spans
    owner_ids = jnp.arange(spans, dtype=jnp.int32)
    counts = base + half * (owner_ids[None, :] == first[:, None]).astype(jnp.int32) - half * (owner_ids[None, :] == second[:, None]).astype(jnp.int32)
    column_end = jnp.cumsum(counts, axis=0)
    column_start = column_end - counts
    row_start = jnp.cumsum(counts, axis=1) - counts
    ranks = jnp.arange(TOK_DEV, dtype=jnp.int32)
    span_of = jnp.sum((column_end.T[:, None, :] <= ranks[None, :, None]).astype(jnp.int32), axis=2)
    owner_grid = jnp.broadcast_to(owner_ids[:, None], (spans, TOK_DEV))
    within = row_start[span_of, owner_grid] + ranks[None, :] - column_start[span_of, owner_grid]
    shuffles = jax.vmap(lambda k: jax.random.permutation(k, TOK_DEV))(jax.random.split(key_c, spans))
    positions = span_of * TOK_DEV + shuffles[span_of, within]
    band_shuffle = jax.vmap(lambda k: jax.random.permutation(k, TOK_DEV))(jax.random.split(key_d, spans))
    token_ids = owner_grid * TOK_DEV + band_shuffle
    order = jnp.zeros((TOK_VIEW,), jnp.int32).at[positions.reshape(-1)].set(token_ids.reshape(-1).astype(jnp.int32))
    return order


def draw_scan_order(key, part):
    keys = jax.random.split(jax.random.fold_in(key, 7), VIEWS)
    return jax.vmap(scan_one_view)(keys).astype(jnp.int32)


def with_spikes(drawn, key, source, target, shards_of, factor):
    def block_of(axis_at):
        return (jnp.arange(drawn.shape[axis_at]) // (drawn.shape[axis_at] // shards_of)).reshape((-1,) + (1,) * (drawn.ndim - 1 - axis_at))

    near = jax.random.permutation(key, shards_of)[block_of(target)]
    other_side = (block_of(target) + shards_of // 2) % shards_of
    return jnp.where((block_of(source) == near) | (block_of(source) == other_side), factor * drawn, drawn)


def block_scale(stream_key, dims, cuts, smallest, top_value):
    factor_of, own = 1.0, jax.random.fold_in(stream_key, 6)
    for position, parts in cuts:
        heights = jnp.exp(jax.random.uniform(jax.random.fold_in(own, position), (parts,), jnp.float32, smallest / len(cuts), top_value / len(cuts)))
        factor_of = factor_of * jnp.repeat(heights, dims[position] // parts).reshape([-1 if axis == position else 1 for axis in range(len(dims))])
    return factor_of


def bell_draw(stream_key, extent, spread, reach, cuts=(), kind=jnp.bfloat16):
    entries = spread * jax.random.normal(stream_key, extent, jnp.float32)
    if cuts:
        entries = entries * block_scale(stream_key, extent, cuts, -0.22, 0.18)
    return jnp.clip(entries, -reach, reach).astype(kind)


def bell_draw_with(rng, shape, width, bound, shards, heavy, kind=jnp.bfloat16):
    entries = width * jax.random.normal(rng, shape, jnp.float32)
    if shards:
        entries = entries * block_scale(rng, shape, shards, -0.22, 0.18)
    return jnp.clip(with_spikes(entries, jax.random.fold_in(rng, 3), *heavy), -bound, bound).astype(kind)


def setup_inputs(seed: int = 0) -> dict:
    key_of = jax.random.split(jax.random.key(seed), 6)
    tokens = bell_draw_with(key_of[0], (VIEWS, TOK_VIEW, DM), 1.0, 6.0, ((0, 8), (1, 4)), (1, 2, 4, 2.0))
    scan_order = draw_scan_order(jax.random.fold_in(key_of[5], 71), 0)
    w_merge = bell_draw(key_of[2], (MERGE_IN, DO), MERGE_IN ** -0.5, 0.09375)
    bias = bell_draw(key_of[3], (DO,), 1.0, 4.0)
    cotangent = bell_draw(key_of[4], (VIEWS, MTOK_VIEW, DO), 1.0, 6.0, ((0, 8), (1, 4)))
    return dict(tokens=tokens, scan_order=scan_order, w_merge=w_merge, bias=bias, cotangent=cotangent)


def one_view(w_merge, bias, order, feats, grads):
    raster = jnp.zeros((TOK_VIEW, DM), jnp.bfloat16).at[order].set(feats)
    merged = raster.reshape(ROWS // 2, 2, COLS // 2, 2, DM).transpose(0, 2, 1, 3, 4).reshape(MTOK_VIEW, MERGE_IN)
    merged_out = (jnp.dot(merged, w_merge, preferred_element_type=jnp.float32) + bias.astype(jnp.float32)).astype(jnp.bfloat16)
    grad_merged = lax.dot_general(grads, w_merge, (((1,), (1,)), ((), ())), preferred_element_type=jnp.float32).astype(jnp.bfloat16)
    grad_raster = grad_merged.reshape(ROWS // 2, COLS // 2, 2, 2, DM).transpose(0, 2, 1, 3, 4).reshape(TOK_VIEW, DM)
    token_grad = grad_raster[order]
    weight_part = lax.dot_general(merged, grads, (((0,), (0,)), ((), ())), preferred_element_type=jnp.float32)
    return (merged_out, token_grad, weight_part)

def reference(tokens, scan_order, w_merge, bias, cotangent):

    def step(carry, items):
        order, feats, grads = items
        merged_out, token_grad, weight_part = one_view(w_merge, bias, order, feats, grads)
        return (carry + weight_part, (merged_out, token_grad))
    start = jnp.zeros((MERGE_IN, DO), jnp.float32)
    weight_sum, stacked = lax.scan(step, start, (scan_order, tokens, cotangent))
    scale = 1.0 / math.sqrt(VIEWS * MTOK_VIEW)
    bias_grad = lax.optimization_barrier(jnp.sum(cotangent.astype(jnp.float32), axis=(0, 1))) * scale
    return (stacked[0], stacked[1], weight_sum * scale, bias_grad)
```

```python
import functools
import math

import jax
import jax.numpy as jnp
from jax import lax
from jax.experimental import pallas as pl
from jax.experimental.pallas import tpu as pltpu
from jax.sharding import PartitionSpec as P

COLS = 128
MERGE = 4
LANES = 128


def general_body(tokens, scan_order, w_merge, bias, cotangent):
    spans = lax.axis_size("span")
    views = lax.axis_size("view")
    span_index = lax.axis_index("span")
    tok_dev = tokens.shape[1]
    width = tokens.shape[2]
    capacity = 3 * (tok_dev // spans) // 2
    rows_dev = tok_dev // COLS
    order_all = scan_order[0].reshape(spans, tok_dev)
    owners = order_all // tok_dev
    owner_hot = (owners[:, :, None] == jnp.arange(spans, dtype=jnp.int32)[None, None, :]).astype(
        jnp.int32
    )
    slot_rank = jnp.sum((jnp.cumsum(owner_hot, axis=1) - 1) * owner_hot, axis=2)
    dest_slots = owners * capacity + slot_rank
    my_slots = lax.dynamic_index_in_dim(dest_slots, span_index, 0, keepdims=False)
    outgoing = jnp.zeros((spans * capacity, width), jnp.bfloat16).at[my_slots].set(tokens[0])
    received = lax.all_to_all(
        outgoing.reshape(spans, capacity, width), "span", split_axis=0, concat_axis=0, tiled=True
    )
    arriving = owners == span_index
    source_slot = jnp.arange(spans, dtype=jnp.int32)[:, None] * capacity + slot_rank
    local_index = jnp.where(arriving, order_all - span_index * tok_dev, tok_dev)
    source_of = (
        jnp.zeros((tok_dev,), jnp.int32)
        .at[local_index.reshape(-1)]
        .set(source_slot.reshape(-1), mode="drop")
    )
    raster = received.reshape(spans * capacity, width)[source_of]
    merged = (
        raster.reshape(rows_dev // 2, 2, COLS // 2, 2, width)
        .transpose(0, 2, 1, 3, 4)
        .reshape(tok_dev // 4, 4 * width)
    )
    merged_out = (
        jnp.dot(merged, w_merge, preferred_element_type=jnp.float32) + bias.astype(jnp.float32)
    ).astype(jnp.bfloat16)
    grads = cotangent[0]
    grad_merged = lax.dot_general(
        grads, w_merge, (((1,), (1,)), ((), ())), preferred_element_type=jnp.float32
    ).astype(jnp.bfloat16)
    grad_raster = (
        grad_merged.reshape(rows_dev // 2, COLS // 2, 2, 2, width)
        .transpose(0, 2, 1, 3, 4)
        .reshape(tok_dev, width)
    )
    going_back = jnp.zeros((spans * capacity, width), jnp.bfloat16).at[source_of].set(grad_raster)
    returned = lax.all_to_all(
        going_back.reshape(spans, capacity, width), "span", split_axis=0, concat_axis=0, tiled=True
    )
    token_grad = returned.reshape(spans * capacity, width)[my_slots]
    kernel_rows = 4 * width
    merged_rows = merged.shape[0]
    group_rows = kernel_rows // (views * spans)
    regrouped = merged.reshape(merged_rows, views, spans, group_rows).transpose(0, 2, 1, 3)
    view_tokens = lax.all_to_all(regrouped, "span", split_axis=1, concat_axis=0, tiled=True)
    view_tokens = view_tokens.reshape(spans * merged_rows, views * group_rows)
    all_grads = lax.all_gather(grads, "span", axis=0, tiled=True)
    partial_sum = lax.dot_general(
        view_tokens, all_grads, (((0,), (0,)), ((), ())), preferred_element_type=jnp.float32
    )
    weight_sum = lax.psum_scatter(partial_sum, "view", scatter_dimension=0, tiled=True)
    bias_total = lax.psum(jnp.sum(grads.astype(jnp.float32), axis=0), ("view", "span"))
    grad_scale = 1.0 / math.sqrt(views * spans * (tok_dev // 4))
    return (merged_out[None], token_grad[None], weight_sum * grad_scale, bias_total * grad_scale)


def xor_permute(x, axis, offset):
    n = lax.axis_size(axis)
    return lax.ppermute(x, axis, [(i, i ^ offset) for i in range(n)])


def raster_of(k, band, local, tok_dev):
    half = COLS // 2
    row = local // half
    col = local % half
    return band * tok_dev + (2 * row + k // 2) * COLS + 2 * col + k % 2


def order_row(order_ref, block):
    return order_ref[pl.ds(block, 1), :]


def bf16_hot(mask):
    return jnp.where(mask, 1.0, 0.0).astype(jnp.bfloat16)


def select_kernel(order_ref, t0, tx, ty, tda, tdb, m0, m1, m2, m3):
    spans, tok_dev = order_ref.shape
    mrows = tok_dev // MERGE
    s = lax.axis_index("span")
    z = lax.axis_index("view") // 2
    half = tda.shape[0]
    orders = [order_row(order_ref, s ^ o) for o in range(spans)]
    order = jnp.concatenate(orders, axis=1)
    group = LANES
    stride = spans * group

    def channels(ref):
        return jnp.concatenate(
            [ref[:, pl.ds(pl.multiple_of(s * group + c * stride, group), group)] for c in range(2)],
            axis=1,
        )

    slab = jnp.concatenate([channels(r) for r in (t0, tx, ty, tda, tdb)], axis=0)
    target = lax.broadcasted_iota(jnp.int32, (tok_dev, 1), 0)
    band = s ^ (target // mrows)
    local = target % mrows
    for dz, out in enumerate((m0, m1, m2, m3)):
        raster = raster_of(z ^ dz, band, local, tok_dev)
        hot = bf16_hot(raster == order)
        out[...] = jnp.dot(hot, slab, preferred_element_type=jnp.float32).astype(jnp.bfloat16)


def main_kernel(order_ref, t0, tx, ty, tda, tdb, c0, cx, cy, cda, cdb, w_ref, bias_ref, out, tgrad):
    spans, tok_dev = order_ref.shape
    width = t0.shape[1]
    mrows = tok_dev // MERGE
    s = lax.axis_index("span")
    half = tda.shape[0]
    local = lax.broadcasted_iota(jnp.int32, (tok_dev, 1), 0)
    raster = raster_of(local // mrows, s, local % mrows, tok_dev)
    orders = [order_row(order_ref, s ^ o) for o in range(spans)]
    order = jnp.concatenate(orders, axis=1)
    tokens = jnp.concatenate([r[...] for r in (t0, tx, ty, tda, tdb)], axis=0)
    mine = jnp.dot(
        bf16_hot(raster == order), tokens, preferred_element_type=jnp.float32
    ).astype(jnp.bfloat16)
    grads = jnp.concatenate([r[...] for r in (c0, cx, cy, cda, cdb)], axis=0)
    target = lax.broadcasted_iota(jnp.int32, (tok_dev, 1), 0)
    band = s ^ (target // mrows)
    acc = bias_ref[...].astype(jnp.float32)
    tacc = None
    for k in range(MERGE):
        w_k = w_ref[k * width:(k + 1) * width, :]
        acc = acc + jnp.dot(
            mine[k * mrows:(k + 1) * mrows, :], w_k, preferred_element_type=jnp.float32
        )
        hot = bf16_hot(raster_of(k, band, target % mrows, tok_dev) == orders[0])
        picked = lax.dot_general(
            hot, grads, (((0,), (0,)), ((), ())), preferred_element_type=jnp.float32
        ).astype(jnp.bfloat16)
        term = lax.dot_general(
            picked, w_k, (((1,), (1,)), ((), ())), preferred_element_type=jnp.float32
        )
        tacc = term if tacc is None else tacc + term
    out[...] = acc.astype(jnp.bfloat16)
    tgrad[...] = tacc.astype(jnp.bfloat16)


def weight_kernel(m0, m1, m2, m3, c0, e0, cx, ex, cy, ey, cda, cdb, eda, edb, keep, give):
    mrows = c0.shape[0]
    core = lax.axis_index("view") % 2
    f32 = jnp.float32

    def stacked(o):
        return jnp.concatenate(
            [m[o * mrows:(o + 1) * mrows, :] for m in (m0, m2, m1, m3)], axis=0
        )

    blocks = [(c0, e0), (cx, ex), (cy, ey), (cda, cdb, eda, edb)]
    lhs = jnp.concatenate([stacked(o) for o in range(len(blocks))], axis=0)
    rhs = jnp.concatenate([r[...] for b in blocks for r in b], axis=0)
    group = lhs.shape[1] // 2
    total = lax.dot_general(lhs, rhs, (((0,), (0,)), ((), ())), preferred_element_type=f32)
    low, high = total[:group], total[group:]
    mine = core == 0
    keep[:group, :] = jnp.where(mine, low, high)
    give[:group, :] = jnp.where(mine, high, low)
    pieces = rhs.astype(f32).reshape(len(blocks), 4, mrows, rhs.shape[1])

    def block_sum(b):
        return (b[0] + b[2]) + (b[1] + b[3])

    sums = [block_sum(pieces[o]) for o in range(len(blocks))]
    tree = (sums[0] + sums[1]) + (sums[2] + sums[3])
    bias = jnp.sum(tree, axis=0, keepdims=True)
    keep[group:, :] = jnp.broadcast_to(bias, (8, bias.shape[1]))
    give[group:, :] = jnp.broadcast_to(bias, (8, bias.shape[1]))


def call(kernel, args, outs):
    vmem = pl.BlockSpec(memory_space=pltpu.VMEM)
    return pl.pallas_call(
        kernel,
        out_shape=outs,
        in_specs=[vmem] * len(args),
        out_specs=[vmem] * len(outs),
        compiler_params=pltpu.CompilerParams(vmem_limit_bytes=40 * 1024 * 1024),
    )(*args)


def quad_body(tokens, scan_order, w_merge, bias, cotangent):
    spans = lax.axis_size("span")
    views = lax.axis_size("view")
    tok_dev = tokens.shape[1]
    width = tokens.shape[2]
    mrows = tok_dev // MERGE
    group = MERGE * width // (views * spans)
    order = scan_order[0].reshape(spans, tok_dev)
    t0 = tokens[0]
    c0 = cotangent[0]
    hop_x = functools.partial(xor_permute, axis="span", offset=1)
    hop_y = functools.partial(xor_permute, axis="span", offset=2)

    def hop_z(x, dz):
        return xor_permute(x, "view", 2 * dz)

    def gather(x):
        half = x.shape[0] // 2
        px, py = hop_x(x), hop_y(x)
        return px, py, hop_y(px[:half]), hop_x(py[half:])

    c2 = hop_z(c0, 2)
    cs = gather(c0)
    ts = gather(t0)
    c13 = hop_z(jnp.concatenate([c0, c2], axis=0), 1)
    extra = jnp.concatenate([c2, c13], axis=0)
    es = gather(extra)

    bf16 = jnp.bfloat16
    f32 = jnp.float32
    picks = call(
        select_kernel,
        (order, t0, *ts),
        [jax.ShapeDtypeStruct((tok_dev, 2 * group), bf16)] * MERGE,
    )
    ms = [picks[0]] + [hop_z(picks[dz], dz) for dz in range(1, MERGE)]
    merged_out, token_grad = call(
        main_kernel,
        (order, t0, *ts, c0, *cs, w_merge, bias.reshape(1, -1)),
        [
            jax.ShapeDtypeStruct((mrows, width), bf16),
            jax.ShapeDtypeStruct((tok_dev, width), bf16),
        ],
    )
    keep, give = call(
        weight_kernel,
        (*ms, c0, extra, cs[0], es[0], cs[1], es[1], cs[2], cs[3], es[2], es[3]),
        [jax.ShapeDtypeStruct((group + 8, width), f32)] * 2,
    )
    taken = xor_permute(give, "view", 1)
    total = (keep + taken) * (1.0 / math.sqrt(views * spans * mrows))
    return merged_out[None], token_grad[None], total[:group], total[group]


def body(tokens, scan_order, w_merge, bias, cotangent):
    spans = lax.axis_size("span")
    views = lax.axis_size("view")
    width = tokens.shape[2]
    group = MERGE * width // (views * spans)
    if spans == 4 and views == 2 * MERGE and group == LANES:
        return quad_body(tokens, scan_order, w_merge, bias, cotangent)
    return general_body(tokens, scan_order, w_merge, bias, cotangent)


def solution(mesh):
    in_specs = (P("view", "span", None), P("view", None), P(), P(), P("view", "span", None))
    out_specs = (P("view", "span", None), P("view", "span", None), P(("view", "span"), None), P())
    return jax.shard_map(body, mesh=mesh, in_specs=in_specs, out_specs=out_specs, check_vma=False)
```

```python
import functools
import math

import jax
import jax.numpy as jnp
from jax import lax
from jax.experimental import pallas as pl
from jax.experimental.pallas import tpu as pltpu
from jax.sharding import PartitionSpec as P


COLS = 128
MERGE = 4
SPANS = 4
LANES = 128
PACK_LIMIT = 32
MAIN_LIMIT = 52


def general_body(tokens, scan_order, w_merge, bias, cotangent):
    spans = lax.axis_size("span")
    views = lax.axis_size("view")
    span_index = lax.axis_index("span")
    tok_dev = tokens.shape[1]
    width = tokens.shape[2]
    capacity = 3 * (tok_dev // spans) // 2
    rows_dev = tok_dev // COLS
    order_all = scan_order[0].reshape(spans, tok_dev)
    owners = order_all // tok_dev
    owner_hot = (owners[:, :, None] == jnp.arange(spans, dtype=jnp.int32)[None, None, :]).astype(
        jnp.int32
    )
    slot_rank = jnp.sum((jnp.cumsum(owner_hot, axis=1) - 1) * owner_hot, axis=2)
    dest_slots = owners * capacity + slot_rank
    my_slots = lax.dynamic_index_in_dim(dest_slots, span_index, 0, keepdims=False)
    outgoing = jnp.zeros((spans * capacity, width), jnp.bfloat16).at[my_slots].set(tokens[0])
    received = lax.all_to_all(
        outgoing.reshape(spans, capacity, width), "span", split_axis=0, concat_axis=0, tiled=True
    )
    arriving = owners == span_index
    source_slot = jnp.arange(spans, dtype=jnp.int32)[:, None] * capacity + slot_rank
    local_index = jnp.where(arriving, order_all - span_index * tok_dev, tok_dev)
    source_of = (
        jnp.zeros((tok_dev,), jnp.int32)
        .at[local_index.reshape(-1)]
        .set(source_slot.reshape(-1), mode="drop")
    )
    raster = received.reshape(spans * capacity, width)[source_of]
    merged = (
        raster.reshape(rows_dev // 2, 2, COLS // 2, 2, width)
        .transpose(0, 2, 1, 3, 4)
        .reshape(tok_dev // 4, 4 * width)
    )
    merged_out = (
        jnp.dot(merged, w_merge, preferred_element_type=jnp.float32) + bias.astype(jnp.float32)
    ).astype(jnp.bfloat16)
    grads = cotangent[0]
    grad_merged = lax.dot_general(
        grads, w_merge, (((1,), (1,)), ((), ())), preferred_element_type=jnp.float32
    ).astype(jnp.bfloat16)
    grad_raster = (
        grad_merged.reshape(rows_dev // 2, COLS // 2, 2, 2, width)
        .transpose(0, 2, 1, 3, 4)
        .reshape(tok_dev, width)
    )
    going_back = jnp.zeros((spans * capacity, width), jnp.bfloat16).at[source_of].set(grad_raster)
    returned = lax.all_to_all(
        going_back.reshape(spans, capacity, width), "span", split_axis=0, concat_axis=0, tiled=True
    )
    token_grad = returned.reshape(spans * capacity, width)[my_slots]
    kernel_rows = 4 * width
    merged_rows = merged.shape[0]
    group_rows = kernel_rows // (views * spans)
    regrouped = merged.reshape(merged_rows, views, spans, group_rows).transpose(0, 2, 1, 3)
    view_tokens = lax.all_to_all(regrouped, "span", split_axis=1, concat_axis=0, tiled=True)
    view_tokens = view_tokens.reshape(spans * merged_rows, views * group_rows)
    all_grads = lax.all_gather(grads, "span", axis=0, tiled=True)
    partial_sum = lax.dot_general(
        view_tokens, all_grads, (((0,), (0,)), ((), ())), preferred_element_type=jnp.float32
    )
    weight_sum = lax.psum_scatter(partial_sum, "view", scatter_dimension=0, tiled=True)
    bias_total = lax.psum(jnp.sum(grads.astype(jnp.float32), axis=0), ("view", "span"))
    grad_scale = 1.0 / math.sqrt(views * spans * (tok_dev // 4))
    return (merged_out[None], token_grad[None], weight_sum * grad_scale, bias_total * grad_scale)


def xor_permute(x, axis, offset):
    n = lax.axis_size(axis)
    return lax.ppermute(x, axis, [(i, i ^ offset) for i in range(n)])


def raster_of(k, band, local, tok_dev):
    half = COLS // 2
    row = local // half
    col = local % half
    return band * tok_dev + (2 * row + k // 2) * COLS + 2 * col + k % 2


def order_row(order_ref, block, tok_dev):
    return order_ref[:, pl.ds(pl.multiple_of(block * tok_dev, LANES), tok_dev)]


def bf16_hot(mask):
    return jnp.where(mask, 1.0, 0.0).astype(jnp.bfloat16)


def rank_of(member):
    n = member.shape[1]
    upper = lax.broadcasted_iota(jnp.int32, (n, n), 0) <= lax.broadcasted_iota(jnp.int32, (n, n), 1)
    rows = jnp.broadcast_to(bf16_hot(member), (16, n))
    count = jnp.dot(rows, bf16_hot(upper), preferred_element_type=jnp.float32)
    return count[:1].astype(jnp.int32) - 1


def slot_hot(order, band, tok_dev, slots):
    member = (order // tok_dev) == band
    slot = lax.broadcasted_iota(jnp.int32, (slots, order.shape[1]), 0)
    return jnp.where(member & (rank_of(member) == slot), 1.0, 0.0).astype(jnp.bfloat16)


def pack_kernel(order_hbm, t_hbm, c_hbm, b_hbm, order_ref, t_ref, c_ref, b_ref, x1, x2, x3, p1, p2, p3,
                sems):
    tok_dev = t_ref.shape[0]
    mrows = c_ref.shape[0]
    group = LANES
    s = lax.axis_index("span")
    stride = group * SPANS
    pairs = ((order_hbm, order_ref), (t_hbm, t_ref), (c_hbm, c_ref), (b_hbm, b_ref))
    copies = [pltpu.make_async_copy(a, b, sems.at[i]) for i, (a, b) in enumerate(pairs)]
    for copy in copies:
        copy.start()
    for copy in copies:
        copy.wait()
    x1[:mrows, :] = c_ref[...]
    x2[:mrows, :] = c_ref[...]
    for o, x, first in ((1, x1, mrows), (2, x2, mrows), (3, x3, 0)):
        for c in range(2):
            start = pl.multiple_of((s ^ o) * group + c * stride, LANES)
            for j in range(MERGE):
                column = (2 * j + c) * group
                x[first:first + mrows, column:column + group] = t_ref[
                    j * mrows:(j + 1) * mrows, pl.ds(start, group)
                ]
    order = order_row(order_ref, s, tok_dev)
    for o, p in ((1, p1), (2, p2), (3, p3)):
        hot = slot_hot(order, s ^ o, tok_dev, p.shape[0])
        p[...] = jnp.dot(hot, t_ref[...], preferred_element_type=jnp.float32).astype(p.dtype)


def select_kernel(order_ref, t_ref, x1, x2, x3, m0, m1, m2, m3):
    tok_dev = t_ref.shape[0]
    mrows = tok_dev // MERGE
    group = LANES
    stride = group * SPANS
    s = lax.axis_index("span")
    z = lax.axis_index("view") // 2
    order = jnp.concatenate([order_row(order_ref, s ^ o, tok_dev) for o in range(SPANS)], axis=1)
    starts = [pl.multiple_of(s * group + c * stride, LANES) for c in range(2)]
    parts = [jnp.concatenate([t_ref[:, pl.ds(start, group)] for start in starts], axis=1)]
    for x, first in ((x1, mrows), (x2, mrows), (x3, 0)):
        parts += [
            x[first:first + mrows, 2 * j * group:2 * (j + 1) * group] for j in range(MERGE)
        ]
    slab = jnp.concatenate(parts, axis=0)
    target = lax.broadcasted_iota(jnp.int32, (tok_dev, 1), 0)
    band = s ^ (target // mrows)
    local = target % mrows
    for dz, out in enumerate((m0, m1, m2, m3)):
        raster = raster_of(z ^ dz, band, local, tok_dev)
        hot = bf16_hot(raster == order)
        out[...] = jnp.dot(hot, slab, preferred_element_type=jnp.float32).astype(out.dtype)


def fetch(w_hbm, w_ref, sems, k):
    width = w_ref.shape[1]
    rows = pl.ds(pl.multiple_of(k * width, width), width)
    return pltpu.make_async_copy(w_hbm.at[rows, :], w_ref.at[k], sems.at[k])


def forward_kernel(order_ref, bias_ref, t_ref, p1, p2, p3, w_hbm, out, mine_ref, acc_ref, w_ref, sems):
    tok_dev = t_ref.shape[0]
    mrows = tok_dev // MERGE
    s = lax.axis_index("span")
    f32 = jnp.float32
    for k in range(MERGE):
        fetch(w_hbm, w_ref, sems, k).start()
    local = lax.broadcasted_iota(jnp.int32, (tok_dev, 1), 0)
    raster = raster_of(local // mrows, s, local % mrows, tok_dev)
    mine_order = order_row(order_ref, s, tok_dev)
    mine = jnp.dot(bf16_hot(raster == mine_order), t_ref[...], preferred_element_type=f32)
    key = raster - s * tok_dev + 1
    for o, p in ((1, p1), (2, p2), (3, p3)):
        order = order_row(order_ref, s ^ o, tok_dev)
        slots = slot_hot(order, s, tok_dev, p.shape[0])
        place = jnp.where(order // tok_dev == s, order - s * tok_dev + 1, 0)
        place = jnp.broadcast_to(place, (16, tok_dev)).astype(f32).astype(jnp.bfloat16)
        held = lax.dot_general(place, slots, (((1,), (1,)), ((), ())), preferred_element_type=f32)
        hot = bf16_hot(key == held[:1].astype(jnp.int32))
        mine += jnp.dot(hot, p[...], preferred_element_type=f32)
    mine_ref[...] = mine.astype(mine_ref.dtype)
    acc_ref[...] = jnp.broadcast_to(bias_ref[...].astype(f32).reshape(1, -1), acc_ref.shape)

    @pl.loop(0, MERGE)
    def _(k):
        fetch(w_hbm, w_ref, sems, k).wait()
        rows = mine_ref[pl.ds(pl.multiple_of(k * mrows, mrows), mrows), :]
        acc_ref[...] += jnp.dot(rows, w_ref[k], preferred_element_type=f32)

    out[...] = acc_ref[...].astype(out.dtype)


def backward_kernel(order_ref, c0, x1, x2, cda, cdb, w_hbm, tgrad, grads_ref, tacc_ref, w_ref, sems):
    mrows = c0.shape[0]
    tok_dev = MERGE * mrows
    s = lax.axis_index("span")
    f32 = jnp.float32
    for k in range(MERGE):
        fetch(w_hbm, w_ref, sems, k).start()
    grads_ref[...] = jnp.concatenate(
        [c0[...], x1[:mrows, :], x2[:mrows, :], cda[...], cdb[...]], axis=0
    )
    tacc_ref[...] = jnp.zeros_like(tacc_ref)
    local = lax.broadcasted_iota(jnp.int32, (tok_dev, 1), 0)
    band = s ^ (local // mrows)
    order = order_row(order_ref, s, tok_dev)

    @pl.loop(0, MERGE)
    def _(k):
        hot = bf16_hot(raster_of(k, band, local % mrows, tok_dev) == order)
        picked = lax.dot_general(
            hot, grads_ref[...], (((0,), (0,)), ((), ())), preferred_element_type=f32
        ).astype(jnp.bfloat16)
        fetch(w_hbm, w_ref, sems, k).wait()
        tacc_ref[...] += lax.dot_general(
            picked, w_ref[k], (((1,), (1,)), ((), ())), preferred_element_type=f32
        )

    tgrad[...] = tacc_ref[...].astype(tgrad.dtype)


def weight_kernel(m0, m1, m2, m3, c0, e0, x1, ex, x2, ey, cda, cdb, eda, edb, keep, keep_bias, give):
    mrows = c0.shape[0]
    core = lax.axis_index("view") % 2
    f32 = jnp.float32

    def stacked(o):
        return jnp.concatenate(
            [m[o * mrows:(o + 1) * mrows, :] for m in (m0, m2, m1, m3)], axis=0
        )

    cx, cy = x1.at[:mrows], x2.at[:mrows]
    blocks = [(c0, e0), (cx, ex), (cy, ey), (cda, cdb, eda, edb)]
    lhs = jnp.concatenate([stacked(o) for o in range(len(blocks))], axis=0)
    rhs = jnp.concatenate([r[...] for b in blocks for r in b], axis=0)
    group = lhs.shape[1] // 2
    total = lax.dot_general(lhs, rhs, (((0,), (0,)), ((), ())), preferred_element_type=f32)
    low, high = total[:group], total[group:]
    mine = core == 0
    keep[...] = jnp.where(mine, low, high)
    give[:group, :] = jnp.where(mine, high, low)
    pieces = rhs.astype(f32).reshape(len(blocks), MERGE, mrows, rhs.shape[1])

    def block_sum(b):
        return (b[0] + b[2]) + (b[1] + b[3])

    sums = [block_sum(pieces[o]) for o in range(len(blocks))]
    tree = (sums[0] + sums[1]) + (sums[2] + sums[3])
    bias = jnp.broadcast_to(jnp.sum(tree, axis=0, keepdims=True), keep_bias.shape)
    keep_bias[...] = bias
    give[group:, :] = bias


def finish_kernel(scale, keep, keep_bias, taken, weight_grad, bias_grad):
    group = keep.shape[0]
    weight_grad[...] = (keep[...] + taken[:group, :]) * scale
    bias_grad[...] = (keep_bias[:1, :] + taken[group:group + 1, :]) * scale


def shape(rows, cols, dtype=jnp.bfloat16):
    return jax.ShapeDtypeStruct((rows, cols), dtype)


def call(kernel, args, outs, cost, hbm=(), scratch=(), limit=32):
    vmem = pl.BlockSpec(memory_space=pltpu.VMEM)
    far = pl.BlockSpec(memory_space=pltpu.HBM)
    return pl.pallas_call(
        kernel,
        out_shape=outs,
        in_specs=[far if i in hbm else vmem for i in range(len(args))],
        out_specs=[vmem] * len(outs),
        scratch_shapes=scratch,
        cost_estimate=cost,
        compiler_params=pltpu.CompilerParams(vmem_limit_bytes=int(limit * 1024 * 1024)),
    )(*args)


def cost_of(flops, moved):
    return pl.CostEstimate(flops=flops, bytes_accessed=moved, transcendentals=0)


def quad_steps(tokens, scan_order, w_merge, bias, cotangent):
    spans = lax.axis_size("span")
    views = lax.axis_size("view")
    tok_dev = tokens.shape[1]
    width = tokens.shape[2]
    mrows = tok_dev // MERGE
    group = MERGE * width // (views * spans)
    capacity = 3 * (tok_dev // spans) // 2
    f32 = jnp.float32
    t0 = tokens[0]
    c0 = cotangent[0]

    half = mrows // 2
    bf16 = jnp.bfloat16
    order, tv, cv, bv, *sent = call(
        pack_kernel,
        (scan_order, t0, c0, bias),
        [
            shape(*scan_order.shape, jnp.int32),
            shape(tok_dev, width),
            shape(mrows, width),
            jax.ShapeDtypeStruct(bias.shape, bias.dtype),
        ]
        + [shape(2 * mrows, width)] * 2
        + [shape(mrows, width)]
        + [shape(capacity, width)] * 3,
        cost_of(2 * 3 * capacity * tok_dev * width, 4 * tok_dev * width),
        hbm=(0, 1, 2, 3),
        scratch=[pltpu.SemaphoreType.DMA((4,))],
        limit=PACK_LIMIT,
    )
    x1, x2, x3 = [xor_permute(sent[o - 1], "span", o) for o in range(1, 4)]
    c2 = xor_permute(c0, "view", 4)
    ps = [xor_permute(sent[o + 2], "span", o) for o in range(1, 4)]
    c13 = xor_permute(jnp.concatenate([cv, c2], axis=0), "view", 2)
    extra = jnp.concatenate([c2, c13], axis=0)
    cda = xor_permute(x1[:half], "span", 2)
    cdb = xor_permute(x2[half:mrows], "span", 1)
    ex = xor_permute(extra, "span", 1)
    ey = xor_permute(extra, "span", 2)
    ehalf = extra.shape[0] // 2
    eda = xor_permute(ex[:ehalf], "span", 2)
    edb = xor_permute(ey[ehalf:], "span", 1)
    picks = call(
        select_kernel,
        (order, tv, x1, x2, x3),
        [shape(tok_dev, 2 * group)] * MERGE,
        cost_of(2 * spans * spans * tok_dev * tok_dev * 2 * group, 4 * tok_dev * width),
    )
    ms = [picks[0]] + [xor_permute(picks[dz], "view", 2 * dz) for dz in range(1, MERGE)]
    weights = [pltpu.VMEM((MERGE, width, width), bf16), pltpu.SemaphoreType.DMA((MERGE,))]
    (merged_out,) = call(
        forward_kernel,
        (order, bv, tv, *ps, w_merge),
        [shape(mrows, width)],
        cost_of(4 * tok_dev * width * width, 8 * width * width),
        hbm=(6,),
        scratch=[pltpu.VMEM((tok_dev, width), bf16), pltpu.VMEM((mrows, width), f32)] + weights,
        limit=MAIN_LIMIT,
    )
    (token_grad,) = call(
        backward_kernel,
        (order, cv, x1, x2, cda, cdb, w_merge),
        [shape(tok_dev, width)],
        cost_of(10 * tok_dev * width * width, 8 * width * width),
        hbm=(6,),
        scratch=[pltpu.VMEM((tok_dev, width), bf16), pltpu.VMEM((tok_dev, width), f32)] + weights,
        limit=MAIN_LIMIT,
    )
    keep, keep_bias, give = call(
        weight_kernel,
        (*ms, cv, extra, x1, ex, x2, ey, cda, cdb, eda, edb),
        [shape(group, width, f32), shape(8, width, f32), shape(group + 8, width, f32)],
        cost_of(4 * spans * tok_dev * group * width, 8 * tok_dev * width),
    )
    taken = xor_permute(give, "view", 1)
    scale = 1.0 / math.sqrt(views * spans * mrows)
    weight_grad, bias_grad = call(
        functools.partial(finish_kernel, scale),
        (keep, keep_bias, taken),
        [shape(group, width, f32), shape(1, width, f32)],
        cost_of(group * width, 12 * group * width),
    )
    return merged_out[None], token_grad[None], weight_grad, bias_grad[0]


def body(tokens, scan_order, w_merge, bias, cotangent):
    spans = lax.axis_size("span")
    views = lax.axis_size("view")
    width = tokens.shape[2]
    group = MERGE * width // (views * spans)
    if spans == SPANS and views == 2 * MERGE and group == LANES:
        return quad_steps(tokens, scan_order, w_merge, bias, cotangent)
    return general_body(tokens, scan_order, w_merge, bias, cotangent)


def solution(mesh):
    in_specs = (P("view", "span", None), P("view", None), P(), P(), P("view", "span", None))
    out_specs = (P("view", "span", None), P("view", "span", None), P(("view", "span"), None), P())
    return jax.shard_map(body, mesh=mesh, in_specs=in_specs, out_specs=out_specs, check_vma=False)
```

```python
import functools
import math

import jax
import jax.numpy as jnp
from jax import lax
from jax.experimental import pallas as pl
from jax.experimental.pallas import tpu as pltpu
from jax.sharding import PartitionSpec as P


COLS = 128
MERGE = 4
SPANS = 4
LANES = 128
MAIN_LIMIT = 44


def general_body(tokens, scan_order, w_merge, bias, cotangent):
    spans = lax.axis_size("span")
    views = lax.axis_size("view")
    span_index = lax.axis_index("span")
    tok_dev = tokens.shape[1]
    width = tokens.shape[2]
    capacity = 3 * (tok_dev // spans) // 2
    rows_dev = tok_dev // COLS
    order_all = scan_order[0].reshape(spans, tok_dev)
    owners = order_all // tok_dev
    owner_hot = (owners[:, :, None] == jnp.arange(spans, dtype=jnp.int32)[None, None, :]).astype(
        jnp.int32
    )
    slot_rank = jnp.sum((jnp.cumsum(owner_hot, axis=1) - 1) * owner_hot, axis=2)
    dest_slots = owners * capacity + slot_rank
    my_slots = lax.dynamic_index_in_dim(dest_slots, span_index, 0, keepdims=False)
    outgoing = jnp.zeros((spans * capacity, width), jnp.bfloat16).at[my_slots].set(tokens[0])
    received = lax.all_to_all(
        outgoing.reshape(spans, capacity, width), "span", split_axis=0, concat_axis=0, tiled=True
    )
    arriving = owners == span_index
    source_slot = jnp.arange(spans, dtype=jnp.int32)[:, None] * capacity + slot_rank
    local_index = jnp.where(arriving, order_all - span_index * tok_dev, tok_dev)
    source_of = (
        jnp.zeros((tok_dev,), jnp.int32)
        .at[local_index.reshape(-1)]
        .set(source_slot.reshape(-1), mode="drop")
    )
    raster = received.reshape(spans * capacity, width)[source_of]
    merged = (
        raster.reshape(rows_dev // 2, 2, COLS // 2, 2, width)
        .transpose(0, 2, 1, 3, 4)
        .reshape(tok_dev // 4, 4 * width)
    )
    merged_out = (
        jnp.dot(merged, w_merge, preferred_element_type=jnp.float32) + bias.astype(jnp.float32)
    ).astype(jnp.bfloat16)
    grads = cotangent[0]
    grad_merged = lax.dot_general(
        grads, w_merge, (((1,), (1,)), ((), ())), preferred_element_type=jnp.float32
    ).astype(jnp.bfloat16)
    grad_raster = (
        grad_merged.reshape(rows_dev // 2, COLS // 2, 2, 2, width)
        .transpose(0, 2, 1, 3, 4)
        .reshape(tok_dev, width)
    )
    going_back = jnp.zeros((spans * capacity, width), jnp.bfloat16).at[source_of].set(grad_raster)
    returned = lax.all_to_all(
        going_back.reshape(spans, capacity, width), "span", split_axis=0, concat_axis=0, tiled=True
    )
    token_grad = returned.reshape(spans * capacity, width)[my_slots]
    kernel_rows = 4 * width
    merged_rows = merged.shape[0]
    group_rows = kernel_rows // (views * spans)
    regrouped = merged.reshape(merged_rows, views, spans, group_rows).transpose(0, 2, 1, 3)
    view_tokens = lax.all_to_all(regrouped, "span", split_axis=1, concat_axis=0, tiled=True)
    view_tokens = view_tokens.reshape(spans * merged_rows, views * group_rows)
    all_grads = lax.all_gather(grads, "span", axis=0, tiled=True)
    partial_sum = lax.dot_general(
        view_tokens, all_grads, (((0,), (0,)), ((), ())), preferred_element_type=jnp.float32
    )
    weight_sum = lax.psum_scatter(partial_sum, "view", scatter_dimension=0, tiled=True)
    bias_total = lax.psum(jnp.sum(grads.astype(jnp.float32), axis=0), ("view", "span"))
    grad_scale = 1.0 / math.sqrt(views * spans * (tok_dev // 4))
    return (merged_out[None], token_grad[None], weight_sum * grad_scale, bias_total * grad_scale)


def xor_permute(x, view_offset, span_offset):
    views, spans = lax.axis_size("view"), lax.axis_size("span")
    pairs = []
    for i in range(views * spans):
        view, span = divmod(i, spans)
        step = span_offset[view % 2] if span_offset else 0
        pairs.append((i, (view ^ view_offset) * spans + (span ^ step)))
    return lax.ppermute(x, ("view", "span"), pairs)


def raster_of(k, band, local, tok_dev):
    half = COLS // 2
    row = local // half
    col = local % half
    return band * tok_dev + (2 * row + k // 2) * COLS + 2 * col + k % 2


def order_row(order_ref, block, tok_dev):
    return order_ref[:, pl.ds(pl.multiple_of(block * tok_dev, LANES), tok_dev)]


def bf16_hot(mask):
    return jnp.where(mask, 1.0, 0.0).astype(jnp.bfloat16)


def rank_of(member):
    n = member.shape[1]
    upper = lax.broadcasted_iota(jnp.int32, (n, n), 0) <= lax.broadcasted_iota(jnp.int32, (n, n), 1)
    rows = jnp.broadcast_to(bf16_hot(member), (16, n))
    count = jnp.dot(rows, bf16_hot(upper), preferred_element_type=jnp.float32)
    return count[:1].astype(jnp.int32) - 1


def slot_hot(order, band, tok_dev, slots):
    member = (order // tok_dev) == band
    slot = lax.broadcasted_iota(jnp.int32, (slots, order.shape[1]), 0)
    return jnp.where(member & (rank_of(member) == slot), 1.0, 0.0).astype(jnp.bfloat16)


def band_offsets():
    core = lax.axis_index("view") % 2
    return (0, 1 + core, 2 - core, 3)


def band_of(block, s):
    offset = jnp.zeros_like(block)
    for j, o in enumerate(band_offsets()):
        offset = jnp.where(block == j, o, offset)
    return s ^ offset


def channel_starts(s, group):
    return [pl.multiple_of(s * group + c * SPANS * group, LANES) for c in range(2)]


def pack_kernel(order_ref, t_in, t_ref, q_first, q_second, p_first, p_second):
    tok_dev = t_in.shape[0]
    mrows = tok_dev // MERGE
    slots = p_second.shape[0] // 2
    group = LANES
    s = lax.axis_index("span")
    _, h, g, d = band_offsets()
    t_ref[...] = t_in[...]
    for o, q, first in ((h, q_first, 0), (d, q_first, mrows), (g, q_second, 0)):
        for c, start in enumerate(channel_starts(s ^ o, group)):
            for j in range(MERGE):
                column = (2 * j + c) * group
                q[first:first + mrows, column:column + group] = t_in[
                    j * mrows:(j + 1) * mrows, pl.ds(start, group)
                ]
    order = order_row(order_ref, s, tok_dev)
    for o, p, first in ((h, p_first, 0), (d, p_first, slots), (g, p_second, 0)):
        hot = slot_hot(order, s ^ o, tok_dev, slots)
        rows = jnp.dot(hot, t_in[...], preferred_element_type=jnp.float32)
        p[first:first + slots, :] = rows.astype(p.dtype)


def hold_kernel(c_ref, c_out):
    c_out[:c_ref.shape[0], :] = c_ref[...]


def stage_kernel(first, w_hbm, *refs):
    *outs, sems = refs
    width = outs[0].shape[0]
    copies = []
    for i, out in enumerate(outs):
        rows = pl.ds((first + i) * width, width)
        copies.append(pltpu.make_async_copy(w_hbm.at[rows, :], out, sems.at[i]))
        copies[-1].start()
    for copy in copies:
        copy.wait()


def select_kernel(order_ref, t_ref, q_near, q_far, m0, m1, m2, m3):
    tok_dev = t_ref.shape[0]
    mrows = tok_dev // MERGE
    group = LANES
    s = lax.axis_index("span")
    z = lax.axis_index("view") // 2
    order = jnp.concatenate([order_row(order_ref, s ^ o, tok_dev) for o in band_offsets()], axis=1)
    mine = [t_ref[:, pl.ds(start, group)] for start in channel_starts(s, group)]
    parts = [jnp.concatenate(mine, axis=1)]
    for q, first in ((q_near, 0), (q_far, 0), (q_far, mrows)):
        parts += [
            q[first:first + mrows, 2 * j * group:2 * (j + 1) * group] for j in range(MERGE)
        ]
    slab = jnp.concatenate(parts, axis=0)
    target = lax.broadcasted_iota(jnp.int32, (tok_dev, 1), 0)
    band = band_of(target // mrows, s)
    local = target % mrows
    for dz, out in enumerate((m0, m1, m2, m3)):
        raster = raster_of(z ^ dz, band, local, tok_dev)
        hot = bf16_hot(raster == order)
        out[...] = jnp.dot(hot, slab, preferred_element_type=jnp.float32).astype(out.dtype)


def forward_kernel(order_ref, bias_ref, t_ref, p_near, p_far, w0, w1, w2, w3, out):
    tok_dev = t_ref.shape[0]
    mrows = tok_dev // MERGE
    slots = p_far.shape[0] // 2
    s = lax.axis_index("span")
    _, h, g, d = band_offsets()
    f32 = jnp.float32
    local = lax.broadcasted_iota(jnp.int32, (tok_dev, 1), 0)
    raster = raster_of(local // mrows, s, local % mrows, tok_dev)
    mine_order = order_row(order_ref, s, tok_dev)
    mine = jnp.dot(bf16_hot(raster == mine_order), t_ref[...], preferred_element_type=f32)
    key = raster - s * tok_dev + 1
    for o, p, first in ((h, p_near, 0), (g, p_far, 0), (d, p_far, slots)):
        order = order_row(order_ref, s ^ o, tok_dev)
        held = slot_hot(order, s, tok_dev, slots)
        place = jnp.where(order // tok_dev == s, order - s * tok_dev + 1, 0)
        place = jnp.broadcast_to(place, (16, tok_dev)).astype(f32).astype(jnp.bfloat16)
        held = lax.dot_general(place, held, (((1,), (1,)), ((), ())), preferred_element_type=f32)
        hot = bf16_hot(key == held[:1].astype(jnp.int32))
        mine += jnp.dot(hot, p[first:first + slots, :], preferred_element_type=f32)
    mine = mine.astype(jnp.bfloat16)
    acc = bias_ref[...].astype(f32).reshape(1, -1)
    for k, w in enumerate((w0, w1, w2, w3)):
        rows = mine[k * mrows:(k + 1) * mrows, :]
        acc = acc + jnp.dot(rows, w[...], preferred_element_type=f32)
    out[...] = acc.astype(out.dtype)


def backward_kernel(order_ref, near, far, w0, w1, w2, w3, tgrad):
    mrows = near.shape[0] // 2
    tok_dev = MERGE * mrows
    s = lax.axis_index("span")
    f32 = jnp.float32
    grads = jnp.concatenate([near[...], far[...]], axis=0)
    local = lax.broadcasted_iota(jnp.int32, (tok_dev, 1), 0)
    band = band_of(local // mrows, s)
    order = order_row(order_ref, s, tok_dev)
    hots = []
    rasters = []
    for k, w in enumerate((w0, w1, w2, w3)):
        hots.append(bf16_hot(raster_of(k, band, local % mrows, tok_dev) == order))
        rasters.append(
            lax.dot_general(
                grads, w[...], (((1,), (1,)), ((), ())), preferred_element_type=f32
            ).astype(jnp.bfloat16)
        )
    tgrad[...] = lax.dot_general(
        jnp.concatenate(hots, axis=0),
        jnp.concatenate(rasters, axis=0),
        (((0,), (0,)), ((), ())),
        preferred_element_type=f32,
    ).astype(tgrad.dtype)


def weight_kernel(m0, m1, m2, m3, cnear, cfar, e0, e1, e2, e3, keep, keep_bias, give):
    mrows = cnear.shape[0] // 2
    core = lax.axis_index("view") % 2
    f32 = jnp.float32

    def stacked(j):
        return jnp.concatenate(
            [m[j * mrows:(j + 1) * mrows, :] for m in (m0, m1, m2, m3)], axis=0
        )

    lhs = jnp.concatenate([stacked(j) for j in range(SPANS)], axis=0)
    blocks = []
    for c, pair in ((cnear, (e0, e1)), (cfar, (e2, e3))):
        for j, e in enumerate(pair):
            blocks += [c[j * mrows:(j + 1) * mrows, :], e[...]]
    rhs = jnp.concatenate(blocks, axis=0)
    group = lhs.shape[1] // 2
    total = lax.dot_general(lhs, rhs, (((0,), (0,)), ((), ())), preferred_element_type=f32)
    low, high = total[:group], total[group:]
    mine = core == 0
    keep[...] = jnp.where(mine, low, high)
    give[:group, :] = jnp.where(mine, high, low)
    pieces = rhs.astype(f32).reshape(SPANS, MERGE, mrows, rhs.shape[1])

    def block_sum(b):
        return (b[0] + b[1]) + (b[2] + b[3])

    sums = [block_sum(pieces[j]) for j in range(SPANS)]
    tree = (sums[0] + sums[1]) + (sums[2] + sums[3])
    bias = jnp.broadcast_to(jnp.sum(tree, axis=0, keepdims=True), keep_bias.shape)
    keep_bias[...] = bias
    give[group:, :] = bias


def finish_kernel(scale, keep, keep_bias, taken, weight_grad, bias_grad):
    group = keep.shape[0]
    weight_grad[...] = (keep[...] + taken[:group, :]) * scale
    bias_grad[...] = (keep_bias[:1, :] + taken[group:group + 1, :]) * scale


def shape(rows, cols, dtype=jnp.bfloat16):
    return jax.ShapeDtypeStruct((rows, cols), dtype)


def call(kernel, args, outs, cost, hbm=(), scratch=(), limit=32):
    vmem = pl.BlockSpec(memory_space=pltpu.VMEM)
    far = pl.BlockSpec(memory_space=pltpu.HBM)
    return pl.pallas_call(
        kernel,
        out_shape=outs,
        in_specs=[far if i in hbm else vmem for i in range(len(args))],
        out_specs=[vmem] * len(outs),
        scratch_shapes=scratch,
        cost_estimate=cost,
        compiler_params=pltpu.CompilerParams(vmem_limit_bytes=int(limit * 1024 * 1024)),
    )(*args)


def cost_of(flops, moved):
    return pl.CostEstimate(flops=flops, bytes_accessed=moved, transcendentals=0)


def join_rows(buffer, tail):
    return lax.dynamic_update_slice(buffer, tail, (buffer.shape[0] - tail.shape[0], 0))


def quad_steps(tokens, scan_order, w_merge, bias, cotangent):
    spans = lax.axis_size("span")
    views = lax.axis_size("view")
    tok_dev = tokens.shape[1]
    width = tokens.shape[2]
    mrows = tok_dev // MERGE
    group = MERGE * width // (views * spans)
    f32 = jnp.float32
    t0 = tokens[0]
    c0 = cotangent[0]

    def hop(x, view_offset=0, span_offset=None):
        return xor_permute(x, view_offset, span_offset)

    first, second = (1, 2), (2, 1)
    capacity = 3 * (tok_dev // spans) // 2
    c1 = hop(c0, span_offset=first)
    zs = [hop(c0, view_offset=2 * dz) for dz in range(1, MERGE)]
    tv, q_first, q_second, p_first, p_second = call(
        pack_kernel,
        (scan_order, t0),
        [
            shape(tok_dev, width),
            shape(2 * mrows, width),
            shape(2 * mrows, width),
            shape(2 * capacity, width),
            shape(2 * capacity, width),
        ],
        cost_of(2 * 3 * capacity * tok_dev * width, 4 * tok_dev * width),
    )
    q_near = hop(q_first, span_offset=first)
    p_near = hop(p_first, span_offset=first)
    (c_half,) = call(
        hold_kernel, (c0,), [shape(2 * mrows, width)], cost_of(width, 4 * mrows * width)
    )
    q_far = hop(join_rows(q_second, q_near[mrows:]), span_offset=second)
    p_far = hop(join_rows(p_second, p_near[capacity:]), span_offset=second)
    cnear = join_rows(c_half, c1)
    cfar = hop(cnear, span_offset=second)
    extra = jnp.concatenate(zs, axis=0)
    e1 = hop(extra, span_offset=first)
    e2 = hop(extra, span_offset=second)
    e3 = hop(e1, span_offset=second)
    picks = call(
        select_kernel,
        (scan_order, tv, q_near, q_far),
        [shape(tok_dev, 2 * group)] * MERGE,
        cost_of(2 * spans * spans * tok_dev * tok_dev * 2 * group, 4 * tok_dev * width),
    )
    ms = [picks[0]] + [hop(picks[dz], view_offset=2 * dz) for dz in range(1, MERGE)]
    weights = []
    for first in range(0, MERGE, 2):
        weights += call(
            functools.partial(stage_kernel, first),
            (w_merge,),
            [shape(width, width)] * 2,
            cost_of(width, 4 * width * width),
            hbm=(0,),
            scratch=[pltpu.SemaphoreType.DMA((2,))],
            limit=MAIN_LIMIT,
        )
    (token_grad,) = call(
        backward_kernel,
        (scan_order, cnear, cfar, *weights),
        [shape(tok_dev, width)],
        cost_of(10 * tok_dev * width * width, 8 * width * width),
    )
    (merged_out,) = call(
        forward_kernel,
        (scan_order, bias, tv, p_near, p_far, *weights),
        [shape(mrows, width)],
        cost_of(4 * tok_dev * width * width, 8 * width * width),
    )
    keep, keep_bias, give = call(
        weight_kernel,
        (*ms, cnear, cfar, extra, e1, e2, e3),
        [shape(group, width, f32), shape(8, width, f32), shape(group + 8, width, f32)],
        cost_of(4 * spans * tok_dev * group * width, 8 * tok_dev * width),
    )
    taken = hop(give, view_offset=1)
    scale = 1.0 / math.sqrt(views * spans * mrows)
    weight_grad, bias_grad = call(
        functools.partial(finish_kernel, scale),
        (keep, keep_bias, taken),
        [shape(group, width, f32), shape(1, width, f32)],
        cost_of(group * width, 12 * group * width),
    )
    return merged_out[None], token_grad[None], weight_grad, bias_grad[0]


def body(tokens, scan_order, w_merge, bias, cotangent):
    spans = lax.axis_size("span")
    views = lax.axis_size("view")
    width = tokens.shape[2]
    group = MERGE * width // (views * spans)
    if spans == SPANS and views == 2 * MERGE and group == LANES:
        return quad_steps(tokens, scan_order, w_merge, bias, cotangent)
    return general_body(tokens, scan_order, w_merge, bias, cotangent)


def solution(mesh):
    in_specs = (P("view", "span", None), P("view", None), P(), P(), P("view", "span", None))
    out_specs = (P("view", "span", None), P("view", "span", None), P(("view", "span"), None), P())
    return jax.shard_map(body, mesh=mesh, in_specs=in_specs, out_specs=out_specs, check_vma=False)
```

```python
import functools
import math

import jax
import jax.numpy as jnp
from jax import lax
from jax.experimental import pallas as pl
from jax.experimental.pallas import tpu as pltpu
from jax.sharding import PartitionSpec as P


COLS = 128
MERGE = 4
SPANS = 4
LANES = 128
MAIN_LIMIT = 44


def general_body(tokens, scan_order, w_merge, bias, cotangent):
    spans = lax.axis_size("span")
    views = lax.axis_size("view")
    span_index = lax.axis_index("span")
    tok_dev = tokens.shape[1]
    width = tokens.shape[2]
    capacity = 3 * (tok_dev // spans) // 2
    rows_dev = tok_dev // COLS
    order_all = scan_order[0].reshape(spans, tok_dev)
    owners = order_all // tok_dev
    owner_hot = (owners[:, :, None] == jnp.arange(spans, dtype=jnp.int32)[None, None, :]).astype(
        jnp.int32
    )
    slot_rank = jnp.sum((jnp.cumsum(owner_hot, axis=1) - 1) * owner_hot, axis=2)
    dest_slots = owners * capacity + slot_rank
    my_slots = lax.dynamic_index_in_dim(dest_slots, span_index, 0, keepdims=False)
    outgoing = jnp.zeros((spans * capacity, width), jnp.bfloat16).at[my_slots].set(tokens[0])
    received = lax.all_to_all(
        outgoing.reshape(spans, capacity, width), "span", split_axis=0, concat_axis=0, tiled=True
    )
    arriving = owners == span_index
    source_slot = jnp.arange(spans, dtype=jnp.int32)[:, None] * capacity + slot_rank
    local_index = jnp.where(arriving, order_all - span_index * tok_dev, tok_dev)
    source_of = (
        jnp.zeros((tok_dev,), jnp.int32)
        .at[local_index.reshape(-1)]
        .set(source_slot.reshape(-1), mode="drop")
    )
    raster = received.reshape(spans * capacity, width)[source_of]
    merged = (
        raster.reshape(rows_dev // 2, 2, COLS // 2, 2, width)
        .transpose(0, 2, 1, 3, 4)
        .reshape(tok_dev // 4, 4 * width)
    )
    merged_out = (
        jnp.dot(merged, w_merge, preferred_element_type=jnp.float32) + bias.astype(jnp.float32)
    ).astype(jnp.bfloat16)
    grads = cotangent[0]
    grad_merged = lax.dot_general(
        grads, w_merge, (((1,), (1,)), ((), ())), preferred_element_type=jnp.float32
    ).astype(jnp.bfloat16)
    grad_raster = (
        grad_merged.reshape(rows_dev // 2, COLS // 2, 2, 2, width)
        .transpose(0, 2, 1, 3, 4)
        .reshape(tok_dev, width)
    )
    going_back = jnp.zeros((spans * capacity, width), jnp.bfloat16).at[source_of].set(grad_raster)
    returned = lax.all_to_all(
        going_back.reshape(spans, capacity, width), "span", split_axis=0, concat_axis=0, tiled=True
    )
    token_grad = returned.reshape(spans * capacity, width)[my_slots]
    kernel_rows = 4 * width
    merged_rows = merged.shape[0]
    group_rows = kernel_rows // (views * spans)
    regrouped = merged.reshape(merged_rows, views, spans, group_rows).transpose(0, 2, 1, 3)
    view_tokens = lax.all_to_all(regrouped, "span", split_axis=1, concat_axis=0, tiled=True)
    view_tokens = view_tokens.reshape(spans * merged_rows, views * group_rows)
    all_grads = lax.all_gather(grads, "span", axis=0, tiled=True)
    partial_sum = lax.dot_general(
        view_tokens, all_grads, (((0,), (0,)), ((), ())), preferred_element_type=jnp.float32
    )
    weight_sum = lax.psum_scatter(partial_sum, "view", scatter_dimension=0, tiled=True)
    bias_total = lax.psum(jnp.sum(grads.astype(jnp.float32), axis=0), ("view", "span"))
    grad_scale = 1.0 / math.sqrt(views * spans * (tok_dev // 4))
    return (merged_out[None], token_grad[None], weight_sum * grad_scale, bias_total * grad_scale)


def xor_permute(x, view_offset, span_offset):
    views, spans = lax.axis_size("view"), lax.axis_size("span")
    pairs = []
    for i in range(views * spans):
        view, span = divmod(i, spans)
        step = span_offset[view % 2] if span_offset else 0
        pairs.append((i, (view ^ view_offset) * spans + (span ^ step)))
    return lax.ppermute(x, ("view", "span"), pairs)


def raster_of(k, band, local, tok_dev):
    half = COLS // 2
    row = local // half
    col = local % half
    return band * tok_dev + (2 * row + k // 2) * COLS + 2 * col + k % 2


def order_row(order_ref, block, tok_dev):
    return order_ref[:, pl.ds(pl.multiple_of(block * tok_dev, LANES), tok_dev)]


def bf16_hot(mask):
    return jnp.where(mask, 1.0, 0.0).astype(jnp.bfloat16)


def rank_of(member):
    n = member.shape[1]
    upper = lax.broadcasted_iota(jnp.int32, (n, n), 0) <= lax.broadcasted_iota(jnp.int32, (n, n), 1)
    rows = jnp.broadcast_to(bf16_hot(member), (16, n))
    count = jnp.dot(rows, bf16_hot(upper), preferred_element_type=jnp.float32)
    return count[:1].astype(jnp.int32) - 1


def slot_hot(order, band, tok_dev, slots):
    member = (order // tok_dev) == band
    slot = lax.broadcasted_iota(jnp.int32, (slots, order.shape[1]), 0)
    return jnp.where(member & (rank_of(member) == slot), 1.0, 0.0).astype(jnp.bfloat16)


def band_offsets():
    core = lax.axis_index("view") % 2
    return (0, 1 + core, 2 - core, 3)


def band_of(block, s):
    offset = jnp.zeros_like(block)
    for j, o in enumerate(band_offsets()):
        offset = jnp.where(block == j, o, offset)
    return s ^ offset


def channel_starts(s, group):
    return [pl.multiple_of(s * group + c * SPANS * group, LANES) for c in range(2)]


def channels_kernel(t_in, t_ref, q_first, q_second):
    tok_dev = t_in.shape[0]
    mrows = tok_dev // MERGE
    group = LANES
    s = lax.axis_index("span")
    _, h, g, d = band_offsets()
    t_ref[...] = t_in[...]
    for o, q, first in ((h, q_first, 0), (d, q_first, mrows), (g, q_second, 0)):
        for c, start in enumerate(channel_starts(s ^ o, group)):
            for j in range(MERGE):
                column = (2 * j + c) * group
                q[first:first + mrows, column:column + group] = t_in[
                    j * mrows:(j + 1) * mrows, pl.ds(start, group)
                ]


def pack_kernel(order_ref, t_ref, p_first, p_second):
    tok_dev = t_ref.shape[0]
    slots = p_second.shape[0] // 2
    s = lax.axis_index("span")
    _, h, g, d = band_offsets()
    order = order_row(order_ref, s, tok_dev)
    for o, p, first in ((h, p_first, 0), (d, p_first, slots), (g, p_second, 0)):
        hot = slot_hot(order, s ^ o, tok_dev, slots)
        rows = jnp.dot(hot, t_ref[...], preferred_element_type=jnp.float32)
        p[first:first + slots, :] = rows.astype(p.dtype)


def hold_kernel(c_ref, c_out):
    c_out[:c_ref.shape[0], :] = c_ref[...]


def stage_kernel(first, w_hbm, *refs):
    *outs, sems = refs
    width = outs[0].shape[0]
    copies = []
    for i, out in enumerate(outs):
        rows = pl.ds((first + i) * width, width)
        copies.append(pltpu.make_async_copy(w_hbm.at[rows, :], out, sems.at[i]))
        copies[-1].start()
    for copy in copies:
        copy.wait()


def select_kernel(order_ref, t_ref, q_near, q_far, m0, m1, m2, m3):
    tok_dev = t_ref.shape[0]
    mrows = tok_dev // MERGE
    group = LANES
    s = lax.axis_index("span")
    z = lax.axis_index("view") // 2
    order = jnp.concatenate([order_row(order_ref, s ^ o, tok_dev) for o in band_offsets()], axis=1)
    mine = [t_ref[:, pl.ds(start, group)] for start in channel_starts(s, group)]
    parts = [jnp.concatenate(mine, axis=1)]
    for q, first in ((q_near, 0), (q_far, 0), (q_far, mrows)):
        parts += [
            q[first:first + mrows, 2 * j * group:2 * (j + 1) * group] for j in range(MERGE)
        ]
    slab = jnp.concatenate(parts, axis=0)
    target = lax.broadcasted_iota(jnp.int32, (tok_dev, 1), 0)
    band = band_of(target // mrows, s)
    local = target % mrows
    for dz, out in enumerate((m0, m1, m2, m3)):
        raster = raster_of(z ^ dz, band, local, tok_dev)
        hot = bf16_hot(raster == order)
        out[...] = jnp.dot(hot, slab, preferred_element_type=jnp.float32).astype(out.dtype)


def place_hot(order_ref, raster, s, o, tok_dev, slots):
    f32 = jnp.float32
    order = order_row(order_ref, s ^ o, tok_dev)
    held = slot_hot(order, s, tok_dev, slots)
    place = jnp.where(order // tok_dev == s, order - s * tok_dev + 1, 0)
    place = jnp.broadcast_to(place, (16, tok_dev)).astype(f32).astype(jnp.bfloat16)
    held = lax.dot_general(place, held, (((1,), (1,)), ((), ())), preferred_element_type=f32)
    return bf16_hot(raster - s * tok_dev + 1 == held[:1].astype(jnp.int32))


def gather_kernel(order_ref, t_ref, p_near, mine_ref, hot_g, hot_d):
    tok_dev = t_ref.shape[0]
    mrows = tok_dev // MERGE
    slots = p_near.shape[0] // 2
    s = lax.axis_index("span")
    _, h, g, d = band_offsets()
    f32 = jnp.float32
    local = lax.broadcasted_iota(jnp.int32, (tok_dev, 1), 0)
    raster = raster_of(local // mrows, s, local % mrows, tok_dev)
    hot = bf16_hot(raster == order_row(order_ref, s, tok_dev))
    near = place_hot(order_ref, raster, s, h, tok_dev, slots)
    mine = jnp.dot(hot, t_ref[...], preferred_element_type=f32)
    mine_ref[...] = mine + jnp.dot(near, p_near[:slots, :], preferred_element_type=f32)
    hot_g[...] = place_hot(order_ref, raster, s, g, tok_dev, slots)
    hot_d[...] = place_hot(order_ref, raster, s, d, tok_dev, slots)


def forward_kernel(bias_ref, mine_ref, hot_g, hot_d, p_far, w0, w1, w2, w3, out):
    mrows = mine_ref.shape[0] // MERGE
    slots = p_far.shape[0] // 2
    f32 = jnp.float32
    mine = mine_ref[...]
    mine += jnp.dot(hot_g[...], p_far[:slots, :], preferred_element_type=f32)
    mine += jnp.dot(hot_d[...], p_far[slots:, :], preferred_element_type=f32)
    mine = mine.astype(jnp.bfloat16)
    acc = bias_ref[...].astype(f32).reshape(1, -1)
    for k, w in enumerate((w0, w1, w2, w3)):
        rows = mine[k * mrows:(k + 1) * mrows, :]
        acc = acc + jnp.dot(rows, w[...], preferred_element_type=f32)
    out[...] = acc.astype(out.dtype)


def backward_kernel(order_ref, near, far, w0, w1, w2, w3, tgrad):
    mrows = near.shape[0] // 2
    tok_dev = MERGE * mrows
    s = lax.axis_index("span")
    f32 = jnp.float32
    grads = jnp.concatenate([near[...], far[...]], axis=0)
    local = lax.broadcasted_iota(jnp.int32, (tok_dev, 1), 0)
    band = band_of(local // mrows, s)
    order = order_row(order_ref, s, tok_dev)
    hots = []
    rasters = []
    for k, w in enumerate((w0, w1, w2, w3)):
        hots.append(bf16_hot(raster_of(k, band, local % mrows, tok_dev) == order))
        rasters.append(
            lax.dot_general(
                grads, w[...], (((1,), (1,)), ((), ())), preferred_element_type=f32
            ).astype(jnp.bfloat16)
        )
    tgrad[...] = lax.dot_general(
        jnp.concatenate(hots, axis=0),
        jnp.concatenate(rasters, axis=0),
        (((0,), (0,)), ((), ())),
        preferred_element_type=f32,
    ).astype(tgrad.dtype)


def split_rows(total):
    group = total.shape[0] // 2
    mine = lax.axis_index("view") % 2 == 0
    low, high = total[:group], total[group:]
    return jnp.where(mine, low, high), jnp.where(mine, high, low)


def early_kernel(m0, m1, m2, m3, cnear, cfar, e0, e1, e2, keep, give, pair, third):
    mrows = cnear.shape[0] // 2
    f32 = jnp.float32
    ms = (m0, m1, m2, m3)
    lhs = []
    rhs = []
    sums = []
    for j, (c, e) in enumerate(((cnear, e0), (cnear, e1), (cfar, e2), (cfar, None))):
        rows = c[(j % 2) * mrows:(j % 2 + 1) * mrows, :]
        count = 1 if e is None else MERGE
        lhs += [m[j * mrows:(j + 1) * mrows, :] for m in ms[:count]]
        rhs.append(rows)
        if e is not None:
            rhs.append(e[...])
            b = [e[i * mrows:(i + 1) * mrows, :].astype(f32) for i in range(MERGE - 1)]
            sums.append((rows.astype(f32) + b[0]) + (b[1] + b[2]))
    total = lax.dot_general(
        jnp.concatenate(lhs, axis=0),
        jnp.concatenate(rhs, axis=0),
        (((0,), (0,)), ((), ())),
        preferred_element_type=f32,
    )
    keep[...], give[...] = split_rows(total)
    pair[...] = sums[0] + sums[1]
    third[...] = sums[2]


def last_rows(ms, theirs, mrows):
    core = lax.axis_index("view") % 2
    group = ms[0].shape[1] // 2
    start = pl.multiple_of((1 - core if theirs else core) * group, LANES)
    first = (SPANS - 1) * mrows
    return jnp.concatenate([m[first:first + mrows, pl.ds(start, group)] for m in ms], axis=0)


def give_kernel(m1, m2, m3, cfar, e3, give_in, pair, third, give, bias_out):
    mrows = cfar.shape[0] // 2
    group = give_in.shape[0]
    f32 = jnp.float32
    give[:group, :] = give_in[...] + lax.dot_general(
        last_rows((m1, m2, m3), True, mrows),
        e3[...],
        (((0,), (0,)), ((), ())),
        preferred_element_type=f32,
    )
    b = [e3[i * mrows:(i + 1) * mrows, :].astype(f32) for i in range(MERGE - 1)]
    fourth = (cfar[mrows:, :].astype(f32) + b[0]) + (b[1] + b[2])
    tree = pair[...] + (third[...] + fourth)
    bias = jnp.broadcast_to(jnp.sum(tree, axis=0, keepdims=True), bias_out.shape)
    bias_out[...] = bias
    give[group:, :] = bias


def keep_kernel(m1, m2, m3, e3, keep_in, keep):
    mrows = e3.shape[0] // (MERGE - 1)
    keep[...] = keep_in[...] + lax.dot_general(
        last_rows((m1, m2, m3), False, mrows),
        e3[...],
        (((0,), (0,)), ((), ())),
        preferred_element_type=jnp.float32,
    )


def finish_kernel(scale, keep, keep_bias, taken, weight_grad, bias_grad):
    group = keep.shape[0]
    weight_grad[...] = (keep[...] + taken[:group, :]) * scale
    bias_grad[...] = (keep_bias[:1, :] + taken[group:group + 1, :]) * scale


def shape(rows, cols, dtype=jnp.bfloat16):
    return jax.ShapeDtypeStruct((rows, cols), dtype)


def call(kernel, args, outs, cost, hbm=(), scratch=(), limit=32):
    vmem = pl.BlockSpec(memory_space=pltpu.VMEM)
    far = pl.BlockSpec(memory_space=pltpu.HBM)
    return pl.pallas_call(
        kernel,
        out_shape=outs,
        in_specs=[far if i in hbm else vmem for i in range(len(args))],
        out_specs=[vmem] * len(outs),
        scratch_shapes=scratch,
        cost_estimate=cost,
        compiler_params=pltpu.CompilerParams(vmem_limit_bytes=int(limit * 1024 * 1024)),
    )(*args)


def cost_of(flops, moved):
    return pl.CostEstimate(flops=flops, bytes_accessed=moved, transcendentals=0)


def join_rows(buffer, tail):
    return lax.dynamic_update_slice(buffer, tail, (buffer.shape[0] - tail.shape[0], 0))


def quad_steps(tokens, scan_order, w_merge, bias, cotangent):
    spans = lax.axis_size("span")
    views = lax.axis_size("view")
    tok_dev = tokens.shape[1]
    width = tokens.shape[2]
    mrows = tok_dev // MERGE
    group = MERGE * width // (views * spans)
    f32 = jnp.float32
    t0 = tokens[0]
    c0 = cotangent[0]

    def hop(x, view_offset=0, span_offset=None):
        return xor_permute(x, view_offset, span_offset)

    first, second = (1, 2), (2, 1)
    capacity = 3 * (tok_dev // spans) // 2
    c1 = hop(c0, span_offset=first)
    zs = [hop(c0, view_offset=2 * dz) for dz in range(1, MERGE)]
    tv, q_first, q_second = call(
        channels_kernel,
        (t0,),
        [shape(tok_dev, width)] + [shape(2 * mrows, width)] * 2,
        cost_of(tok_dev * width, 8 * tok_dev * width),
    )
    p_first, p_second = call(
        pack_kernel,
        (scan_order, tv),
        [shape(2 * capacity, width)] * 2,
        cost_of(2 * 3 * capacity * tok_dev * width, 4 * tok_dev * width),
    )
    q_near = hop(q_first, span_offset=first)
    p_near = hop(p_first, span_offset=first)
    (c_half,) = call(
        hold_kernel, (c0,), [shape(2 * mrows, width)], cost_of(width, 4 * mrows * width)
    )
    q_far = hop(join_rows(q_second, q_near[mrows:]), span_offset=second)
    p_far = hop(join_rows(p_second, p_near[capacity:]), span_offset=second)
    cnear = join_rows(c_half, c1)
    cfar = hop(cnear, span_offset=second)
    extra = jnp.concatenate(zs, axis=0)
    e1 = hop(extra, span_offset=first)
    e2 = hop(extra, span_offset=second)
    e3 = hop(e1, span_offset=second)
    picks = call(
        select_kernel,
        (scan_order, tv, q_near, q_far),
        [shape(tok_dev, 2 * group)] * MERGE,
        cost_of(2 * spans * spans * tok_dev * tok_dev * 2 * group, 4 * tok_dev * width),
    )
    ms = [picks[0]] + [hop(picks[dz], view_offset=2 * dz) for dz in range(1, MERGE)]
    weights = []
    for first in range(0, MERGE, 2):
        weights += call(
            functools.partial(stage_kernel, first),
            (w_merge,),
            [shape(width, width)] * 2,
            cost_of(width, 4 * width * width),
            hbm=(0,),
            scratch=[pltpu.SemaphoreType.DMA((2,))],
            limit=MAIN_LIMIT,
        )
    (token_grad,) = call(
        backward_kernel,
        (scan_order, cnear, cfar, *weights),
        [shape(tok_dev, width)],
        cost_of(10 * tok_dev * width * width, 8 * width * width),
    )
    mine, hot_g, hot_d = call(
        gather_kernel,
        (scan_order, tv, p_near),
        [shape(tok_dev, width, f32)] + [shape(tok_dev, capacity)] * 2,
        cost_of(4 * tok_dev * tok_dev * width, 4 * tok_dev * width),
    )
    (merged_out,) = call(
        forward_kernel,
        (bias, mine, hot_g, hot_d, p_far, *weights),
        [shape(mrows, width)],
        cost_of(4 * tok_dev * width * width, 8 * width * width),
    )
    wide = shape(group, width, f32)
    keep, give, pair, third = call(
        early_kernel,
        (*ms, cnear, cfar, extra, e1, e2),
        [wide, wide] + [shape(mrows, width, f32)] * 2,
        cost_of(4 * spans * tok_dev * group * width, 8 * tok_dev * width),
    )
    give, keep_bias = call(
        give_kernel,
        (*ms[1:], cfar, e3, give, pair, third),
        [shape(group + 8, width, f32), shape(8, width, f32)],
        cost_of(2 * tok_dev * group * width, 4 * tok_dev * width),
    )
    taken = hop(give, view_offset=1)
    (keep,) = call(
        keep_kernel,
        (*ms[1:], e3, keep),
        [wide],
        cost_of(2 * tok_dev * group * width, 4 * tok_dev * width),
    )
    scale = 1.0 / math.sqrt(views * spans * mrows)
    weight_grad, bias_grad = call(
        functools.partial(finish_kernel, scale),
        (keep, keep_bias, taken),
        [shape(group, width, f32), shape(1, width, f32)],
        cost_of(group * width, 12 * group * width),
    )
    return merged_out[None], token_grad[None], weight_grad, bias_grad[0]


def body(tokens, scan_order, w_merge, bias, cotangent):
    spans = lax.axis_size("span")
    views = lax.axis_size("view")
    width = tokens.shape[2]
    group = MERGE * width // (views * spans)
    if spans == SPANS and views == 2 * MERGE and group == LANES:
        return quad_steps(tokens, scan_order, w_merge, bias, cotangent)
    return general_body(tokens, scan_order, w_merge, bias, cotangent)


def solution(mesh):
    in_specs = (P("view", "span", None), P("view", None), P(), P(), P("view", "span", None))
    out_specs = (P("view", "span", None), P("view", "span", None), P(("view", "span"), None), P())
    return jax.shard_map(body, mesh=mesh, in_specs=in_specs, out_specs=out_specs, check_vma=False)
```

```python
import functools
import math

import jax
import jax.numpy as jnp
from jax import lax
from jax.experimental import pallas as pl
from jax.experimental.pallas import tpu as pltpu
from jax.sharding import PartitionSpec as P


COLS = 128
MERGE = 4
SPANS = 4
LANES = 128
MAIN_LIMIT = 44


def general_body(tokens, scan_order, w_merge, bias, cotangent):
    spans = lax.axis_size("span")
    views = lax.axis_size("view")
    span_index = lax.axis_index("span")
    tok_dev = tokens.shape[1]
    width = tokens.shape[2]
    capacity = 3 * (tok_dev // spans) // 2
    rows_dev = tok_dev // COLS
    order_all = scan_order[0].reshape(spans, tok_dev)
    owners = order_all // tok_dev
    owner_hot = (owners[:, :, None] == jnp.arange(spans, dtype=jnp.int32)[None, None, :]).astype(
        jnp.int32
    )
    slot_rank = jnp.sum((jnp.cumsum(owner_hot, axis=1) - 1) * owner_hot, axis=2)
    dest_slots = owners * capacity + slot_rank
    my_slots = lax.dynamic_index_in_dim(dest_slots, span_index, 0, keepdims=False)
    outgoing = jnp.zeros((spans * capacity, width), jnp.bfloat16).at[my_slots].set(tokens[0])
    received = lax.all_to_all(
        outgoing.reshape(spans, capacity, width), "span", split_axis=0, concat_axis=0, tiled=True
    )
    arriving = owners == span_index
    source_slot = jnp.arange(spans, dtype=jnp.int32)[:, None] * capacity + slot_rank
    local_index = jnp.where(arriving, order_all - span_index * tok_dev, tok_dev)
    source_of = (
        jnp.zeros((tok_dev,), jnp.int32)
        .at[local_index.reshape(-1)]
        .set(source_slot.reshape(-1), mode="drop")
    )
    raster = received.reshape(spans * capacity, width)[source_of]
    merged = (
        raster.reshape(rows_dev // 2, 2, COLS // 2, 2, width)
        .transpose(0, 2, 1, 3, 4)
        .reshape(tok_dev // 4, 4 * width)
    )
    merged_out = (
        jnp.dot(merged, w_merge, preferred_element_type=jnp.float32) + bias.astype(jnp.float32)
    ).astype(jnp.bfloat16)
    grads = cotangent[0]
    grad_merged = lax.dot_general(
        grads, w_merge, (((1,), (1,)), ((), ())), preferred_element_type=jnp.float32
    ).astype(jnp.bfloat16)
    grad_raster = (
        grad_merged.reshape(rows_dev // 2, COLS // 2, 2, 2, width)
        .transpose(0, 2, 1, 3, 4)
        .reshape(tok_dev, width)
    )
    going_back = jnp.zeros((spans * capacity, width), jnp.bfloat16).at[source_of].set(grad_raster)
    returned = lax.all_to_all(
        going_back.reshape(spans, capacity, width), "span", split_axis=0, concat_axis=0, tiled=True
    )
    token_grad = returned.reshape(spans * capacity, width)[my_slots]
    kernel_rows = 4 * width
    merged_rows = merged.shape[0]
    group_rows = kernel_rows // (views * spans)
    regrouped = merged.reshape(merged_rows, views, spans, group_rows).transpose(0, 2, 1, 3)
    view_tokens = lax.all_to_all(regrouped, "span", split_axis=1, concat_axis=0, tiled=True)
    view_tokens = view_tokens.reshape(spans * merged_rows, views * group_rows)
    all_grads = lax.all_gather(grads, "span", axis=0, tiled=True)
    partial_sum = lax.dot_general(
        view_tokens, all_grads, (((0,), (0,)), ((), ())), preferred_element_type=jnp.float32
    )
    weight_sum = lax.psum_scatter(partial_sum, "view", scatter_dimension=0, tiled=True)
    bias_total = lax.psum(jnp.sum(grads.astype(jnp.float32), axis=0), ("view", "span"))
    grad_scale = 1.0 / math.sqrt(views * spans * (tok_dev // 4))
    return (merged_out[None], token_grad[None], weight_sum * grad_scale, bias_total * grad_scale)


def xor_permute(x, view_offset, span_offset):
    views, spans = lax.axis_size("view"), lax.axis_size("span")
    pairs = []
    for i in range(views * spans):
        view, span = divmod(i, spans)
        step = span_offset[view % 2] if span_offset else 0
        pairs.append((i, (view ^ view_offset) * spans + (span ^ step)))
    return lax.ppermute(x, ("view", "span"), pairs)


def raster_of(k, band, local, tok_dev):
    half = COLS // 2
    row = local // half
    col = local % half
    return band * tok_dev + (2 * row + k // 2) * COLS + 2 * col + k % 2


def order_row(order_ref, block, tok_dev):
    return order_ref[:, pl.ds(pl.multiple_of(block * tok_dev, LANES), tok_dev)]


def bf16_hot(mask):
    return jnp.where(mask, 1.0, 0.0).astype(jnp.bfloat16)


def rank_of(member):
    n = member.shape[1]
    upper = lax.broadcasted_iota(jnp.int32, (n, n), 0) <= lax.broadcasted_iota(jnp.int32, (n, n), 1)
    rows = jnp.broadcast_to(bf16_hot(member), (16, n))
    count = jnp.dot(rows, bf16_hot(upper), preferred_element_type=jnp.float32)
    return count[:1].astype(jnp.int32) - 1


def slot_hot(order, band, tok_dev, slots):
    member = (order // tok_dev) == band
    slot = lax.broadcasted_iota(jnp.int32, (slots, order.shape[1]), 0)
    return jnp.where(member & (rank_of(member) == slot), 1.0, 0.0).astype(jnp.bfloat16)


def band_offsets():
    core = lax.axis_index("view") % 2
    return (0, 1 + core, 2 - core, 3)


def band_of(block, s):
    offset = jnp.zeros_like(block)
    for j, o in enumerate(band_offsets()):
        offset = jnp.where(block == j, o, offset)
    return s ^ offset


def channel_starts(s, group):
    return [pl.multiple_of(s * group + c * SPANS * group, LANES) for c in range(2)]


def channels_kernel(t_in, t_ref, q_first, q_second):
    tok_dev = t_in.shape[0]
    mrows = tok_dev // MERGE
    group = LANES
    s = lax.axis_index("span")
    _, h, g, d = band_offsets()
    t_ref[...] = t_in[...]
    for o, q, first in ((h, q_first, 0), (d, q_first, mrows), (g, q_second, 0)):
        for c, start in enumerate(channel_starts(s ^ o, group)):
            for j in range(MERGE):
                column = (2 * j + c) * group
                q[first:first + mrows, column:column + group] = t_in[
                    j * mrows:(j + 1) * mrows, pl.ds(start, group)
                ]


def pack_kernel(order_ref, t_ref, p_first, p_second):
    tok_dev = t_ref.shape[0]
    slots = p_second.shape[0] // 2
    s = lax.axis_index("span")
    _, h, g, d = band_offsets()
    order = order_row(order_ref, s, tok_dev)
    for o, p, first in ((h, p_first, 0), (d, p_first, slots), (g, p_second, 0)):
        hot = slot_hot(order, s ^ o, tok_dev, slots)
        rows = jnp.dot(hot, t_ref[...], preferred_element_type=jnp.float32)
        p[first:first + slots, :] = rows.astype(p.dtype)


def hold_kernel(c_ref, c_out):
    c_out[:c_ref.shape[0], :] = c_ref[...]


def stage_kernel(first, w_hbm, *refs):
    *outs, sems = refs
    width = outs[0].shape[0]
    copies = []
    for i, out in enumerate(outs):
        rows = pl.ds((first + i) * width, width)
        copies.append(pltpu.make_async_copy(w_hbm.at[rows, :], out, sems.at[i]))
        copies[-1].start()
    for copy in copies:
        copy.wait()


def select_kernel(order_ref, t_ref, q_near, q_far, m0, m1, m2, m3):
    tok_dev = t_ref.shape[0]
    mrows = tok_dev // MERGE
    group = LANES
    s = lax.axis_index("span")
    z = lax.axis_index("view") // 2
    order = jnp.concatenate([order_row(order_ref, s ^ o, tok_dev) for o in band_offsets()], axis=1)
    mine = [t_ref[:, pl.ds(start, group)] for start in channel_starts(s, group)]
    parts = [jnp.concatenate(mine, axis=1)]
    for q, first in ((q_near, 0), (q_far, 0), (q_far, mrows)):
        parts += [
            q[first:first + mrows, 2 * j * group:2 * (j + 1) * group] for j in range(MERGE)
        ]
    slab = jnp.concatenate(parts, axis=0)
    target = lax.broadcasted_iota(jnp.int32, (tok_dev, 1), 0)
    band = band_of(target // mrows, s)
    local = target % mrows
    for dz, out in enumerate((m0, m1, m2, m3)):
        raster = raster_of(z ^ dz, band, local, tok_dev)
        hot = bf16_hot(raster == order)
        out[...] = jnp.dot(hot, slab, preferred_element_type=jnp.float32).astype(out.dtype)


def place_hot(order_ref, raster, s, o, tok_dev, slots):
    f32 = jnp.float32
    order = order_row(order_ref, s ^ o, tok_dev)
    held = slot_hot(order, s, tok_dev, slots)
    place = jnp.where(order // tok_dev == s, order - s * tok_dev + 1, 0)
    place = jnp.broadcast_to(place, (16, tok_dev)).astype(f32).astype(jnp.bfloat16)
    held = lax.dot_general(place, held, (((1,), (1,)), ((), ())), preferred_element_type=f32)
    return bf16_hot(raster - s * tok_dev + 1 == held[:1].astype(jnp.int32))


def gather_kernel(order_ref, t_ref, p_near, mine_ref, hot_g, hot_d):
    tok_dev = t_ref.shape[0]
    mrows = tok_dev // MERGE
    slots = p_near.shape[0] // 2
    s = lax.axis_index("span")
    _, h, g, d = band_offsets()
    f32 = jnp.float32
    local = lax.broadcasted_iota(jnp.int32, (tok_dev, 1), 0)
    raster = raster_of(local // mrows, s, local % mrows, tok_dev)
    hot = bf16_hot(raster == order_row(order_ref, s, tok_dev))
    near = place_hot(order_ref, raster, s, h, tok_dev, slots)
    mine = jnp.dot(hot, t_ref[...], preferred_element_type=f32)
    mine_ref[...] = mine + jnp.dot(near, p_near[:slots, :], preferred_element_type=f32)
    hot_g[...] = place_hot(order_ref, raster, s, g, tok_dev, slots)
    hot_d[...] = place_hot(order_ref, raster, s, d, tok_dev, slots)


def forward_kernel(bias_ref, mine_ref, hot_g, hot_d, p_far, w0, w1, w2, w3, out):
    mrows = mine_ref.shape[0] // MERGE
    slots = p_far.shape[0] // 2
    f32 = jnp.float32
    mine = mine_ref[...]
    mine += jnp.dot(hot_g[...], p_far[:slots, :], preferred_element_type=f32)
    mine += jnp.dot(hot_d[...], p_far[slots:, :], preferred_element_type=f32)
    mine = mine.astype(jnp.bfloat16)
    acc = bias_ref[...].astype(f32).reshape(1, -1)
    for k, w in enumerate((w0, w1, w2, w3)):
        rows = mine[k * mrows:(k + 1) * mrows, :]
        acc = acc + jnp.dot(rows, w[...], preferred_element_type=f32)
    out[...] = acc.astype(out.dtype)


def backward_kernel(order_ref, near, far, w0, w1, w2, w3, tgrad):
    mrows = near.shape[0] // 2
    tok_dev = MERGE * mrows
    s = lax.axis_index("span")
    f32 = jnp.float32
    grads = jnp.concatenate([near[...], far[...]], axis=0)
    local = lax.broadcasted_iota(jnp.int32, (tok_dev, 1), 0)
    band = band_of(local // mrows, s)
    order = order_row(order_ref, s, tok_dev)
    hots = []
    rasters = []
    for k, w in enumerate((w0, w1, w2, w3)):
        hots.append(bf16_hot(raster_of(k, band, local % mrows, tok_dev) == order))
        rasters.append(
            lax.dot_general(
                grads, w[...], (((1,), (1,)), ((), ())), preferred_element_type=f32
            ).astype(jnp.bfloat16)
        )
    tgrad[...] = lax.dot_general(
        jnp.concatenate(hots, axis=0),
        jnp.concatenate(rasters, axis=0),
        (((0,), (0,)), ((), ())),
        preferred_element_type=f32,
    ).astype(tgrad.dtype)


def split_rows(total):
    group = total.shape[0] // 2
    mine = lax.axis_index("view") % 2 == 0
    low, high = total[:group], total[group:]
    return jnp.where(mine, low, high), jnp.where(mine, high, low)


def early_kernel(m0, m1, m2, m3, cnear, cfar, ez, e0, e1, e2, keep, give, pair, third):
    mrows = cnear.shape[0] // 2
    f32 = jnp.float32
    ms = (m0, m1, m2, m3)
    low, high = pl.ds(0, mrows), pl.ds(mrows, mrows)
    near = [(e0, 0), (e0, 1), (e0, 2)]
    hop = [(e1, 0), (e1, 1), (e1, 2)]
    second = [(e2, 0), (e2, 1), (e2, 2)]
    lhs = []
    rhs = []
    sums = []
    for j, (c, at, parts) in enumerate(
        ((cnear, low, near), (cnear, high, hop), (cfar, low, second), (cfar, high, [(ez, 0)]))
    ):
        blocks = [c[at, :]] + [e[i * mrows:(i + 1) * mrows, :] for e, i in parts]
        lhs += [m[j * mrows:(j + 1) * mrows, :] for m in ms[:len(blocks)]]
        rhs += blocks
        if len(blocks) == MERGE:
            b = [x.astype(f32) for x in blocks]
            sums.append((b[0] + b[1]) + (b[2] + b[3]))
    total = lax.dot_general(
        jnp.concatenate(lhs, axis=0),
        jnp.concatenate(rhs, axis=0),
        (((0,), (0,)), ((), ())),
        preferred_element_type=f32,
    )
    keep[...], give[...] = split_rows(total)
    pair[...] = sums[0] + sums[1]
    third[...] = sums[2]


def last_rows(m2, m3, theirs):
    core = lax.axis_index("view") % 2
    group = m2.shape[1] // 2
    mrows = m2.shape[0] // SPANS
    start = pl.multiple_of((1 - core if theirs else core) * group, LANES)
    first = (SPANS - 1) * mrows
    return jnp.concatenate(
        [m[first:first + mrows, pl.ds(start, group)] for m in (m2, m3)], axis=0
    )


def give_kernel(m2, m3, cfar, ez, e3, give_in, pair, third, give, bias_out):
    mrows = cfar.shape[0] // 2
    group = give_in.shape[0]
    f32 = jnp.float32
    give[:group, :] = give_in[...] + lax.dot_general(
        last_rows(m2, m3, True), e3[...], (((0,), (0,)), ((), ())), preferred_element_type=f32
    )
    b = [e3[i * mrows:(i + 1) * mrows, :].astype(f32) for i in range(2)]
    fourth = (cfar[mrows:, :].astype(f32) + ez[...].astype(f32)) + (b[0] + b[1])
    tree = pair[...] + (third[...] + fourth)
    bias = jnp.broadcast_to(jnp.sum(tree, axis=0, keepdims=True), bias_out.shape)
    bias_out[...] = bias
    give[group:, :] = bias


def keep_kernel(m2, m3, e3, keep_in, keep):
    keep[...] = keep_in[...] + lax.dot_general(
        last_rows(m2, m3, False),
        e3[...],
        (((0,), (0,)), ((), ())),
        preferred_element_type=jnp.float32,
    )


def finish_kernel(scale, keep, keep_bias, taken, weight_grad, bias_grad):
    group = keep.shape[0]
    weight_grad[...] = (keep[...] + taken[:group, :]) * scale
    bias_grad[...] = (keep_bias[:1, :] + taken[group:group + 1, :]) * scale


def shape(rows, cols, dtype=jnp.bfloat16):
    return jax.ShapeDtypeStruct((rows, cols), dtype)


def call(kernel, args, outs, cost, hbm=(), scratch=(), limit=32):
    vmem = pl.BlockSpec(memory_space=pltpu.VMEM)
    far = pl.BlockSpec(memory_space=pltpu.HBM)
    return pl.pallas_call(
        kernel,
        out_shape=outs,
        in_specs=[far if i in hbm else vmem for i in range(len(args))],
        out_specs=[vmem] * len(outs),
        scratch_shapes=scratch,
        cost_estimate=cost,
        compiler_params=pltpu.CompilerParams(vmem_limit_bytes=int(limit * 1024 * 1024)),
    )(*args)


def cost_of(flops, moved):
    return pl.CostEstimate(flops=flops, bytes_accessed=moved, transcendentals=0)


def join_rows(buffer, tail):
    return lax.dynamic_update_slice(buffer, tail, (buffer.shape[0] - tail.shape[0], 0))


def quad_steps(tokens, scan_order, w_merge, bias, cotangent):
    spans = lax.axis_size("span")
    views = lax.axis_size("view")
    tok_dev = tokens.shape[1]
    width = tokens.shape[2]
    mrows = tok_dev // MERGE
    group = MERGE * width // (views * spans)
    f32 = jnp.float32
    t0 = tokens[0]
    c0 = cotangent[0]

    def hop(x, view_offset=0, span_offset=None):
        return xor_permute(x, view_offset, span_offset)

    first, second = (1, 2), (2, 1)
    capacity = 3 * (tok_dev // spans) // 2
    c1 = hop(c0, span_offset=first)
    zs = [hop(c0, view_offset=2 * dz) for dz in range(1, MERGE)]
    tv, q_first, q_second = call(
        channels_kernel,
        (t0,),
        [shape(tok_dev, width)] + [shape(2 * mrows, width)] * 2,
        cost_of(tok_dev * width, 8 * tok_dev * width),
    )
    p_first, p_second = call(
        pack_kernel,
        (scan_order, tv),
        [shape(2 * capacity, width)] * 2,
        cost_of(2 * 3 * capacity * tok_dev * width, 4 * tok_dev * width),
    )
    q_near = hop(q_first, span_offset=first)
    p_near = hop(p_first, span_offset=first)
    (c_half,) = call(
        hold_kernel, (c0,), [shape(2 * mrows, width)], cost_of(width, 4 * mrows * width)
    )
    q_far = hop(join_rows(q_second, q_near[mrows:]), span_offset=second)
    p_far = hop(join_rows(p_second, p_near[capacity:]), span_offset=second)
    cnear = join_rows(c_half, c1)
    cfar = hop(cnear, span_offset=second)
    extra = jnp.concatenate(zs, axis=0)
    e1 = hop(extra, span_offset=first)
    ez = hop(cfar[mrows:], view_offset=2)
    e2 = hop(extra, span_offset=second)
    e3 = hop(e1[mrows:], span_offset=second)
    picks = call(
        select_kernel,
        (scan_order, tv, q_near, q_far),
        [shape(tok_dev, 2 * group)] * MERGE,
        cost_of(2 * spans * spans * tok_dev * tok_dev * 2 * group, 4 * tok_dev * width),
    )
    ms = [picks[0]] + [hop(picks[dz], view_offset=2 * dz) for dz in range(1, MERGE)]
    weights = []
    for first in range(0, MERGE, 2):
        weights += call(
            functools.partial(stage_kernel, first),
            (w_merge,),
            [shape(width, width)] * 2,
            cost_of(width, 4 * width * width),
            hbm=(0,),
            scratch=[pltpu.SemaphoreType.DMA((2,))],
            limit=MAIN_LIMIT,
        )
    (token_grad,) = call(
        backward_kernel,
        (scan_order, cnear, cfar, *weights),
        [shape(tok_dev, width)],
        cost_of(10 * tok_dev * width * width, 8 * width * width),
    )
    mine, hot_g, hot_d = call(
        gather_kernel,
        (scan_order, tv, p_near),
        [shape(tok_dev, width, f32)] + [shape(tok_dev, capacity)] * 2,
        cost_of(4 * tok_dev * tok_dev * width, 4 * tok_dev * width),
    )
    (merged_out,) = call(
        forward_kernel,
        (bias, mine, hot_g, hot_d, p_far, *weights),
        [shape(mrows, width)],
        cost_of(4 * tok_dev * width * width, 8 * width * width),
    )
    wide = shape(group, width, f32)
    keep, give, pair, third = call(
        early_kernel,
        (*ms, cnear, cfar, ez, extra, e1, e2),
        [wide, wide] + [shape(mrows, width, f32)] * 2,
        cost_of(4 * spans * tok_dev * group * width, 8 * tok_dev * width),
    )
    give, keep_bias = call(
        give_kernel,
        (*ms[2:], cfar, ez, e3, give, pair, third),
        [shape(group + 8, width, f32), shape(8, width, f32)],
        cost_of(2 * tok_dev * group * width, 4 * tok_dev * width),
    )
    taken = hop(give, view_offset=1)
    (keep,) = call(
        keep_kernel,
        (*ms[2:], e3, keep),
        [wide],
        cost_of(2 * tok_dev * group * width, 4 * tok_dev * width),
    )
    scale = 1.0 / math.sqrt(views * spans * mrows)
    weight_grad, bias_grad = call(
        functools.partial(finish_kernel, scale),
        (keep, keep_bias, taken),
        [shape(group, width, f32), shape(1, width, f32)],
        cost_of(group * width, 12 * group * width),
    )
    return merged_out[None], token_grad[None], weight_grad, bias_grad[0]


def body(tokens, scan_order, w_merge, bias, cotangent):
    spans = lax.axis_size("span")
    views = lax.axis_size("view")
    width = tokens.shape[2]
    group = MERGE * width // (views * spans)
    if spans == SPANS and views == 2 * MERGE and group == LANES:
        return quad_steps(tokens, scan_order, w_merge, bias, cotangent)
    return general_body(tokens, scan_order, w_merge, bias, cotangent)


def solution(mesh):
    in_specs = (P("view", "span", None), P("view", None), P(), P(), P("view", "span", None))
    out_specs = (P("view", "span", None), P("view", "span", None), P(("view", "span"), None), P())
    return jax.shard_map(body, mesh=mesh, in_specs=in_specs, out_specs=out_specs, check_vma=False)
```
